128 devices in a mesh: dp: 16 (over x, y), owner: 8 (over z, core).
Axes of the slice: x: 4, y: 4, z: 4, core: 2. Of those that a mesh axis runs over, the one named last changes fastest.
Arguments:
- vectors: float32 [96, 262144], P(None, ('dp', 'owner')), as said below
- assignment: int32 [262144], P(('dp', 'owner')), may hold values from 0 to 32767, as said below
- slot: int32 [262144], P(('dp', 'owner')), may hold values from 0 to 15, as said below
- old_centroids: float32 [96, 32768], P(None, ('dp', 'owner')), may hold values from -6 to 6
- prior_counts: int32 [32768], P(('dp', 'owner')), may hold values from 1 to 64
Outputs:
- centroids: float32 [96, 32768], P(None, ('dp', 'owner'))
- rotated: float32 [96, 524288], P(None, ('dp', 'owner'))
The draws below stay inside these ranges and needn't reach their ends.
Inputs may be any that keep to these rules, and one draw needn't show every extreme that they name: `assignment`: the lists owned by one device are 256 consecutive ones in the order of the devices along dp+owner. Of the 2048 vectors of one device, at most 32 name lists of any one device; in every draw some device receives exactly 32 from every device. No two vectors share a list and a slot; in every draw some list has all 16 slots filled. Finite real vectors.
All inputs are finite; a program needn't handle non-finite values.
Results may differ from the reference program's by a relative error of at most 0.0003.
Values sent between devices are 32-bit elements; how exact they have to be, the bound alone decides.
No kernel may reach another device: no remote copies, remote signals or barrier semaphores. Data moves between devices by JAX's collectives and lax.ppermute only.
A program may use at most 128 MiB of HBM per device.

```python
import math
import jax
import jax.numpy as jnp
from jax import lax

D = 96
LIST_DEV = 256
CAP = 16
STEPS = 4
LISTS = 32768
TOK_DEV = 2048
TOKENS = 262144
SEND = 32
N_DP = 16
N_OWNER = 8


def routing(key):
    device_count = TOKENS // TOK_DEV
    cell_count = device_count * SEND
    base = jax.random.fold_in(key, 4242)
    key_heavy, key_bias, key_rank, key_shuffle, key_place = jax.random.split(base, 5)
    heavy = jax.random.randint(key_heavy, (), 0, device_count)
    bias = jax.random.randint(key_bias, (device_count,), 0, cell_count // 2 + 1)
    cell_ids = jnp.arange(cell_count, dtype=jnp.int32)
    cell_owner = cell_ids // SEND
    ranks = jax.vmap(lambda single: jax.random.permutation(single, cell_count))(jax.random.split(key_rank, device_count))
    score = (ranks + bias[cell_owner][None, :]) * cell_count + cell_ids[None, :]
    score = jnp.where((cell_owner == heavy)[None, :], -1 - cell_ids[None, :], score)
    chosen = jnp.argsort(score, axis=1, stable=True)[:, :TOK_DEV].astype(jnp.int32)
    shuffles = jax.vmap(lambda single: jax.random.permutation(single, TOK_DEV))(jax.random.split(key_shuffle, device_count))
    chosen = jnp.take_along_axis(chosen, shuffles, axis=1)
    owner = chosen // SEND
    arrival = jnp.arange(device_count, dtype=jnp.int32)[:, None] * SEND + chosen % SEND
    placement = jax.vmap(lambda single: jax.random.permutation(single, cell_count))(jax.random.split(key_place, device_count))
    local_cell = placement[owner, arrival].astype(jnp.int32)
    assignment = owner * LIST_DEV + local_cell // CAP
    slot_index = local_cell % CAP
    return (owner.reshape(-1), assignment.reshape(-1), slot_index.reshape(-1))


def draw_assignment(key, part):
    return routing(key)[1]


def draw_slot(key, part):
    return routing(key)[2]


def draw_vectors(key, part):
    device_count = TOKENS // TOK_DEV
    owner = routing(key)[0].astype(jnp.float32)
    key_noise, key_rows, key_dims = jax.random.split(jax.random.fold_in(key, 99), 3)
    row_scale = jnp.exp(jax.random.uniform(key_rows, (TOKENS,), jnp.float32, 0.0, math.log(10.0)))
    dim_scale = jnp.exp(jax.random.uniform(key_dims, (D,), jnp.float32, -0.5 * math.log(10.0), 0.5 * math.log(10.0)))
    owner_factor = jnp.sqrt(1.0 + 2.0 * owner / max(device_count - 1, 1))
    noise = jax.random.normal(key_noise, (D, TOKENS), jnp.float32)
    return noise * dim_scale[:, None] * (row_scale * owner_factor)[None, :]


def touch_ends(drawn, key, least, high):
    place = [jax.random.randint(jax.random.fold_in(key, axis), (), 0, length) for axis, length in enumerate(drawn.shape)]
    widest = drawn.shape.index(max(drawn.shape))
    beside = place[:widest] + [(place[widest] + 1) % drawn.shape[widest]] + place[widest + 1:]
    return drawn.at[tuple(place)].set(least).at[tuple(beside)].set(high)


def block_levels(own_key, extent, cuts, least, top_value):
    gain, own = 1.0, jax.random.fold_in(own_key, 6)
    for axis_at, parts in cuts:
        draws = jnp.exp(jax.random.uniform(jax.random.fold_in(own, axis_at), (parts,), jnp.float32, least / len(cuts), top_value / len(cuts)))
        gain = gain * jnp.repeat(draws, extent[axis_at] // parts).reshape([-1 if axis == axis_at else 1 for axis in range(len(extent))])
    return gain


def centred(stream_key, extent, deviation, limit, pieces=(), held_as=jnp.bfloat16):
    values = deviation * jax.random.normal(stream_key, extent, jnp.float32)
    if pieces:
        values = values * block_levels(stream_key, extent, pieces, -0.22, 0.18)
    return jnp.clip(values, -limit, limit).astype(held_as)


def setup_inputs(seed: int = 0) -> dict:
    arg_keys = jax.random.split(jax.random.key(seed), 6)
    vectors = draw_vectors(jax.random.fold_in(arg_keys[5], 71), 0)
    assignment = draw_assignment(jax.random.fold_in(arg_keys[5], 71), 0)
    slot = draw_slot(jax.random.fold_in(arg_keys[5], 71), 0)
    old_centroids = centred(arg_keys[3], (D, LISTS), 1.0, 6.0, ((1, 128),), jnp.float32)
    prior_counts = touch_ends(jax.random.randint(arg_keys[4], (LISTS,), 1, 65), jax.random.fold_in(arg_keys[4], 1), 1, 64).astype(jnp.int32)
    return {"vectors": vectors, "assignment": assignment, "slot": slot, "old_centroids": old_centroids, "prior_counts": prior_counts}


shrink_weight = 0.5
epsilon = 1e-05

def whiten(residual, prior, counts, shrinkage):
    features = residual.shape[0]
    highest = lax.Precision.HIGHEST
    covariance = jnp.einsum('ilc,jlc->ijl', residual, residual, precision=highest)
    identity = jnp.eye(features, dtype=jnp.float32)[:, :, None]
    matrix = (covariance + shrinkage * prior[None, None, :] * identity) / (prior + counts)[None, None, :]
    frobenius = jnp.sqrt(lax.optimization_barrier(jnp.sum(matrix * matrix, axis=(0, 1))))
    root_part = matrix / frobenius[None, None, :]
    inverse_part = jnp.broadcast_to(identity, matrix.shape)
    for repeat in range(STEPS):
        middle = 1.5 * identity - 0.5 * jnp.einsum('ijl,jkl->ikl', inverse_part, root_part, precision=highest)
        root_part = jnp.einsum('ijl,jkl->ikl', root_part, middle, precision=highest)
        inverse_part = jnp.einsum('ijl,jkl->ikl', middle, inverse_part, precision=highest)
    operator = inverse_part / jnp.sqrt(frobenius)[None, None, :]
    return jnp.einsum('ijl,jlc->ilc', operator, residual, precision=highest)

def reference(vectors, assignment, slot, old_centroids, prior_counts):
    slot_total = LISTS * CAP
    target = assignment * CAP + slot
    padded = jnp.zeros((D, slot_total + 1), jnp.float32).at[:, target].set(vectors)[:, :slot_total]
    filled = jnp.zeros((slot_total + 1,), jnp.float32).at[target].set(1.0)[:slot_total]
    shaped = padded.reshape(D, LISTS, CAP)
    occupancy = filled.reshape(LISTS, CAP)
    counts = lax.optimization_barrier(jnp.sum(occupancy, axis=1))
    list_sums = lax.optimization_barrier(jnp.sum(shaped, axis=2))
    prior = prior_counts.astype(jnp.float32)
    centroids = (prior[None, :] * old_centroids + list_sums) / (prior + counts)[None, :]
    residual = shaped - centroids[:, :, None] * occupancy[None, :, :]
    energy = jnp.sum(residual * residual)
    shrinkage = shrink_weight * energy / (D * TOKENS) + epsilon
    flat = residual.reshape(D, slot_total)

    def block(index):
        start = (index * (LIST_DEV * CAP)).astype(jnp.int32)
        piece = lax.dynamic_slice_in_dim(flat, start, LIST_DEV * CAP, 1).reshape(D, LIST_DEV, CAP)
        first = (index * LIST_DEV).astype(jnp.int32)
        prior_piece = lax.dynamic_slice_in_dim(prior, first, LIST_DEV, 0)
        count_piece = lax.dynamic_slice_in_dim(counts, first, LIST_DEV, 0)
        return whiten(piece, prior_piece, count_piece, shrinkage).reshape(D, LIST_DEV * CAP)
    blocks = lax.map(block, jnp.arange(N_DP * N_OWNER, dtype=jnp.int32))
    rotated = jnp.transpose(blocks, (1, 0, 2)).reshape(D, slot_total)
    return (centroids, rotated)
```

```python
import jax
import jax.numpy as jnp
from jax import lax
from jax.experimental import pallas as pl
from jax.experimental.pallas import tpu as pltpu
from jax.sharding import PartitionSpec as P

D = 96
CAP = 16
LISTS = 256
CELLS = LISTS * CAP
TOK = 2048
DEV = 128
SEND = 32
STEPS = 4
AXES = ("dp", "owner")
LANES = 128
TAIL = D - CAP
TOTAL = D * TOK * DEV

shrink_weight = 0.5
epsilon = 1e-05

VMEM = pl.BlockSpec(memory_space=pltpu.VMEM)
BIG = 60 * 1024 * 1024


def dispatch_kernel(vec_ref, assign_ref, slot_ref, send_ref, rows, onehot, pos_v, pos_s, sem):
    f32, bf16, i32 = jnp.float32, jnp.bfloat16, jnp.int32
    chunks = TOK // LANES
    assign = assign_ref[...]
    owner = lax.shift_right_logical(assign, 8)
    here = jnp.bitwise_and(assign, LISTS - 1)
    half = jnp.bitwise_and(here, LANES - 1)
    lane = jnp.bitwise_and(here, LANES) + jnp.bitwise_and(half, 7) * 16 + lax.shift_right_logical(half, 3)
    code = slot_ref[...] * LISTS + lane + 2
    code_high = lax.shift_right_logical(code, 6).astype(f32)
    code_low = jnp.bitwise_and(code, 63).astype(f32)
    sub = lax.broadcasted_iota(i32, (LANES, LANES), 0)
    col = lax.broadcasted_iota(i32, (LANES, LANES), 1)
    for c in range(chunks):
        onehot[c * LANES : (c + 1) * LANES, :] = jnp.where(sub == owner[c : c + 1, :], 1.0, 0.0).astype(bf16)
    before = jnp.concatenate(
        [jnp.where(sub < col, 1.0, 0.0), jnp.ones((LANES, LANES), f32)], axis=1
    ).astype(bf16)
    carry = jnp.zeros((LANES, LANES), f32)
    high = jnp.zeros((LANES, LANES), f32)
    low = jnp.zeros((LANES, LANES), f32)
    lanes_both = (((1,), (1,)), ((), ()))
    for c in range(chunks):
        hot = onehot[c * LANES : (c + 1) * LANES, :]
        counted = jnp.dot(hot, before, preferred_element_type=f32)
        rank = jnp.sum(hot.astype(f32) * (counted[:, :LANES] + carry), axis=0, keepdims=True)
        carry = carry + counted[:, LANES:]
        rank = rank.astype(i32)
        pos_v[c : c + 1, :] = owner[c : c + 1, :] * SEND + rank
        at = sub == rank + D
        high = high + lax.dot_general(
            hot, jnp.where(at, code_high[c : c + 1, :], 0.0).astype(bf16), lanes_both, preferred_element_type=f32
        )
        low = low + lax.dot_general(
            hot, jnp.where(at, code_low[c : c + 1, :], 0.0).astype(bf16), lanes_both, preferred_element_type=f32
        )
    labels = high * 64.0 + low
    labels = jnp.where(labels < 1.0, float(CELLS + 2), labels)
    copy = pltpu.make_async_copy(pos_v, pos_s, sem)
    copy.start()
    fill = jnp.ones((LANES - D, LANES), f32)
    for c in range(chunks):
        block = jnp.concatenate([vec_ref[:, c * LANES : (c + 1) * LANES], fill], axis=0)
        rows[c * LANES : (c + 1) * LANES, :] = block.T
    copy.wait()

    def move(c, carry):
        for t in range(LANES):
            send_ref[pl.ds(pos_s[c, t], 1), :] = rows[pl.ds(c * LANES + t, 1), :]
        return carry

    lax.fori_loop(0, chunks, move, 0)
    lane_row = lax.broadcasted_iota(i32, (1, LANES), 1)
    for d in range(DEV):
        spot = slice(d * SEND, d * SEND + 1)
        send_ref[spot, :] = jnp.where(lane_row >= D, labels[d : d + 1, :], send_ref[spot, :])


def dispatch(vectors, assignment, slot):
    return pl.pallas_call(
        dispatch_kernel,
        out_shape=jax.ShapeDtypeStruct((DEV * SEND, LANES), jnp.float32),
        in_specs=[VMEM] * 3,
        out_specs=VMEM,
        scratch_shapes=[
            pltpu.VMEM((TOK, LANES), jnp.float32),
            pltpu.VMEM((TOK, LANES), jnp.bfloat16),
            pltpu.VMEM((TOK // LANES, LANES), jnp.int32),
            pltpu.SMEM((TOK // LANES, LANES), jnp.int32),
            pltpu.SemaphoreType.DMA,
        ],
        name="dispatch",
    )(vectors, assignment.reshape(TOK // LANES, LANES), slot.reshape(TOK // LANES, LANES))


def place_kernel(got_ref, old_ref, prior_ref, cent_ref, res_ref, stat_ref, energy_ref, cells, lab_v, lab_s, sem):
    f32, i32 = jnp.float32, jnp.int32
    lab_v[...] = got_ref[pl.ds(0, DEV, stride=SEND), :].astype(i32) - 2
    copy = pltpu.make_async_copy(lab_v, lab_s, sem)
    copy.start()
    cells[...] = jnp.zeros(cells.shape, f32)
    copy.wait()

    def move(d, carry):
        for r in range(SEND):
            cells[pl.ds(lab_s[d, D + r], 1), :] = got_ref[pl.ds(d * SEND + r, 1), :]
        return carry

    lax.fori_loop(0, DEV, move, 0)
    lane = lax.broadcasted_iota(i32, (D, LANES), 1)
    to_lane = jnp.bitwise_and(lane, 15) * 8 + lax.shift_right_logical(lane, 4)
    to_list = jnp.bitwise_and(lane, 7) * 16 + lax.shift_right_logical(lane, 3)
    total = jnp.zeros((8, LANES), f32)
    for h in range(LISTS // LANES):
        span = slice(h * LANES, (h + 1) * LANES)
        sums = jnp.zeros((D, LANES), f32)
        counts = jnp.zeros((1, LANES), f32)
        seen = []
        for j in range(CAP):
            start = j * LISTS + h * LANES
            block = cells[start : start + LANES, :].T
            sums = sums + block[:D]
            here = jnp.where(block[D : D + 1] > 0.0, 1.0, 0.0)
            counts = counts + here
            seen.append(here)
            res_ref[j, :, span] = block[:D]
        prior8 = jnp.broadcast_to(prior_ref[:, span].astype(f32), (8, LANES))
        prior = jnp.take_along_axis(prior8, to_lane[:8], axis=1)[:1]
        old = jnp.take_along_axis(old_ref[:, span], to_lane, axis=1)
        weight = prior + counts
        cent = (prior * old + sums) / weight
        cent_ref[:, span] = jnp.take_along_axis(cent, to_list, axis=1)
        stat_ref[:, span] = jnp.concatenate([prior, weight, jnp.zeros((6, LANES), f32)], axis=0)
        for j in range(CAP):
            res = res_ref[j, :, span] - cent * seen[j]
            res_ref[j, :, span] = res
            square = res * res
            for t in range(D // 8):
                total = total + square[8 * t : 8 * t + 8]
    energy_ref[...] = jnp.broadcast_to(jnp.sum(total, axis=0, keepdims=True), (DEV, LANES))


def place(got, old_centroids, prior_counts):
    f32 = jnp.float32
    return pl.pallas_call(
        place_kernel,
        out_shape=(
            jax.ShapeDtypeStruct((D, LISTS), f32),
            jax.ShapeDtypeStruct((CAP, D, LISTS), f32),
            jax.ShapeDtypeStruct((8, LISTS), f32),
            jax.ShapeDtypeStruct((DEV, LANES), f32),
        ),
        in_specs=[VMEM] * 3,
        out_specs=(VMEM,) * 4,
        scratch_shapes=[
            pltpu.VMEM((CELLS + 8, LANES), f32),
            pltpu.VMEM((DEV, LANES), jnp.int32),
            pltpu.SMEM((DEV, LANES), jnp.int32),
            pltpu.SemaphoreType.DMA,
        ],
        name="place",
    )(got, old_centroids, prior_counts.reshape(1, LISTS))


def gram_kernel(res_ref, gram_ref):
    def row(i, carry):
        for h in range(LISTS // LANES):
            span = slice(h * LANES, (h + 1) * LANES)
            left = res_ref[i, :, span]
            for j in range(CAP):
                gram_ref[i, j : j + 1, span] = jnp.sum(left * res_ref[j, :, span], axis=0, keepdims=True)
        return carry

    lax.fori_loop(0, CAP, row, 0)


def gram(res):
    return pl.pallas_call(
        gram_kernel,
        out_shape=jax.ShapeDtypeStruct((CAP, CAP, LISTS), jnp.float32),
        in_specs=[VMEM],
        out_specs=VMEM,
        cost_estimate=pl.CostEstimate(flops=2 * CAP * CAP * D * LISTS, bytes_accessed=4 * CAP * D * LISTS, transcendentals=0),
        name="gram",
    )(res)


def whiten_kernel(res_ref, gram_ref, stat_ref, energy_ref, out_ref, t_ref, m_ref, z_ref, s_ref, o_ref):
    f32, i32 = jnp.float32, jnp.int32
    row_of = lax.broadcasted_iota(i32, (CAP, LISTS), 0)
    energy = jnp.sum(energy_ref[...], axis=(0, 1), keepdims=True)
    shrinkage = shrink_weight * energy / TOTAL + epsilon
    prior = stat_ref[0:1, :]
    weight = stat_ref[1:2, :]
    ridge = shrinkage * prior
    frob = jnp.zeros((CAP, LISTS), f32)
    for i in range(CAP):
        row = (gram_ref[i] + jnp.where(row_of == i, ridge, 0.0)) / weight
        t_ref[i] = row
        frob = frob + row * row
    ridge = ridge / weight
    frob = jnp.sqrt(jnp.sum(frob, axis=0, keepdims=True) + TAIL * (ridge * ridge))

    def times(left, right, into):
        def row(i, carry):
            total = left[i, 0:1, :] * right[0]
            for k in range(1, CAP):
                total = total + left[i, k : k + 1, :] * right[k]
            into[i] = total
            return carry

        lax.fori_loop(0, CAP, row, 0)

    def middle():
        for i in range(CAP):
            m_ref[i] = jnp.where(row_of == i, 1.5, 0.0) - 0.5 * t_ref[i]

    for i in range(CAP):
        t_ref[i] = t_ref[i] / frob
    middle()
    z_ref[...] = m_ref[...]
    for step in range(STEPS - 1):
        times(t_ref, m_ref, s_ref)
        times(s_ref, m_ref, t_ref)
        middle()
        times(m_ref, z_ref, s_ref)
        z_ref[...] = s_ref[...]
    scale = 1.0 / jnp.sqrt(frob)
    for i in range(CAP):
        z_ref[i] = z_ref[i] * scale

    lane = lax.broadcasted_iota(i32, (D, LANES), 1)
    for h in range(LISTS // LANES):
        span = slice(h * LANES, (h + 1) * LANES)

        def apply(j, carry):
            total = res_ref[0, :, span] * z_ref[j, 0:1, span]
            for i in range(1, CAP):
                total = total + res_ref[i, :, span] * z_ref[j, i : i + 1, span]
            o_ref[j] = total
            return carry

        lax.fori_loop(0, CAP, apply, 0)

        def weave(t, carry):
            tile = pl.ds(pl.multiple_of(t * 8, 8), 8)
            parts = [o_ref[j, tile, :] for j in range(CAP)]
            for bit in (8, 4, 2, 1):
                low = jnp.bitwise_and(lane[:8], bit) == 0
                for j in range(CAP):
                    if j & bit == 0:
                        one, two = parts[j], parts[j | bit]
                        parts[j] = jnp.where(low, one, pltpu.roll(two, bit, 1))
                        parts[j | bit] = jnp.where(low, pltpu.roll(one, LANES - bit, 1), two)
            for j in range(CAP):
                at = h * CAP * LANES + j * LANES
                out_ref[tile, at : at + LANES] = parts[j]
            return carry

        lax.fori_loop(0, D // 8, weave, 0)


def whiten(res, gram_blocks, stat, energy):
    f32 = jnp.float32
    return pl.pallas_call(
        whiten_kernel,
        out_shape=jax.ShapeDtypeStruct((D, CELLS), f32),
        in_specs=[VMEM] * 4,
        out_specs=VMEM,
        scratch_shapes=[pltpu.VMEM((CAP, CAP, LISTS), f32)] * 4 + [pltpu.VMEM((CAP, D, LANES), f32)],
        name="whiten",
    )(res, gram_blocks, stat, energy)


def local(vectors, assignment, slot, old_centroids, prior_counts):
    outgoing = dispatch(vectors, assignment, slot).reshape(DEV, SEND, LANES)
    incoming = lax.all_to_all(outgoing, AXES, split_axis=0, concat_axis=0, tiled=True)
    centroids, res, stat, energy = place(incoming.reshape(DEV * SEND, LANES), old_centroids, prior_counts)
    shared = lax.all_to_all(energy.reshape(DEV, 1, LANES), AXES, split_axis=0, concat_axis=0, tiled=True)
    rotated = whiten(res, gram(res), stat, shared.reshape(DEV, LANES))
    return (centroids, rotated)


def solution(mesh):
    placed = (
        P(None, AXES),
        P(AXES),
        P(AXES),
        P(None, AXES),
        P(AXES),
    )
    return jax.shard_map(
        local,
        mesh=mesh,
        in_specs=placed,
        out_specs=(P(None, AXES), P(None, AXES)),
        check_vma=False,
    )
```

```python
import jax
import jax.numpy as jnp
from jax import lax
from jax.experimental import pallas as pl
from jax.experimental.pallas import tpu as pltpu
from jax.sharding import PartitionSpec as P

D = 96
CAP = 16
LISTS = 256
CELLS = LISTS * CAP
TOK = 2048
DEV = 128
SEND = 32
STEPS = 4
AXES = ("dp", "owner")
LANES = 128
TAIL = D - CAP
MAIN = 24
BLOCK = MAIN + 1
TOTAL = D * TOK * DEV

shrink_weight = 0.5
epsilon = 1e-05

VMEM = pl.BlockSpec(memory_space=pltpu.VMEM)
BIG = 60 * 1024 * 1024


def dispatch_kernel(vec_ref, assign_ref, slot_ref, send_ref, rows, stage, pos_v, pos_s, sem):
    f32, bf16, i32 = jnp.float32, jnp.bfloat16, jnp.int32
    wide = 2 * LANES
    assign = assign_ref[...]
    owner = lax.shift_right_logical(assign, 8)
    here = jnp.bitwise_and(assign, LISTS - 1)
    half = jnp.bitwise_and(here, LANES - 1)
    lane = jnp.bitwise_and(here, LANES) + jnp.bitwise_and(half, 7) * 16 + lax.shift_right_logical(half, 3)
    code = slot_ref[...] * LISTS + lane + 1
    code_high = lax.shift_right_logical(code, 6).astype(f32)
    code_low = jnp.bitwise_and(code, 63).astype(f32)

    def pair(x, c):
        return jnp.concatenate([x[2 * c : 2 * c + 1, :], x[2 * c + 1 : 2 * c + 2, :]], axis=1)

    sub = lax.broadcasted_iota(i32, (LANES, wide), 0)
    slots = lax.broadcasted_iota(i32, (SEND, wide), 0)
    row2 = lax.broadcasted_iota(i32, (wide, wide), 0)
    col2 = lax.broadcasted_iota(i32, (wide, wide), 1)
    before = jnp.concatenate([jnp.where(row2 < col2, 1.0, 0.0), jnp.ones((wide, wide), f32)], axis=1).astype(bf16)
    carry = jnp.zeros((LANES, wide), f32)
    codes = jnp.zeros((LANES, 2 * SEND), f32)
    for c in range(TOK // wide):
        mine = pair(owner, c)
        picked = sub == mine
        hot = jnp.where(picked, 1.0, 0.0).astype(bf16)
        counted = jnp.dot(hot, before, preferred_element_type=f32)
        rank = jnp.sum(jnp.where(picked, counted[:, :wide] + carry, 0.0), axis=0, keepdims=True).astype(i32)
        carry = carry + counted[:, wide:]
        pos = jnp.where(rank < MAIN, mine * BLOCK + rank, DEV * BLOCK - MAIN + mine * (SEND - MAIN) + rank)
        pos_v[2 * c : 2 * c + 1, :] = pos[:, :LANES]
        pos_v[2 * c + 1 : 2 * c + 2, :] = pos[:, LANES:]
        at = slots == rank
        marks = jnp.concatenate(
            [jnp.where(at, pair(code_high, c), 0.0), jnp.where(at, pair(code_low, c), 0.0)], axis=0
        ).astype(bf16)
        codes = codes + lax.dot_general(hot, marks, (((1,), (1,)), ((), ())), preferred_element_type=f32)
    copy = pltpu.make_async_copy(pos_v, pos_s, sem)
    copy.start()
    labels = codes[:, :SEND] * 64.0 + codes[:, SEND:] - 1.0
    labels = jnp.where(labels < 0.0, float(CELLS), labels)
    labels = jnp.concatenate([labels, jnp.zeros((DEV, LANES - SEND), f32)], axis=1)
    send_ref[pl.ds(MAIN, DEV, stride=BLOCK), :] = labels
    fill = jnp.zeros((LANES - D, LANES), f32)
    for c in range(TOK // LANES):
        block = jnp.concatenate([vec_ref[:, c * LANES : (c + 1) * LANES], fill], axis=0)
        rows[c * LANES : (c + 1) * LANES, :] = block.T
    copy.wait()
    for c in range(TOK // LANES):
        for t in range(LANES):
            stage[pl.ds(pos_s[c, t], 1), :] = rows[c * LANES + t : c * LANES + t + 1, :]
    outer = lax.broadcasted_iota(i32, (8, LANES), 1) >= D

    def pack(d, carry):
        tail = stage[pl.ds(pl.multiple_of(DEV * BLOCK + 8 * d, 8), 8), :]
        for k in range(MAIN // 8):
            spot = pl.ds(d * BLOCK + 8 * k, 8)
            send_ref[spot, :] = jnp.where(outer, pltpu.roll(tail, D - 32 * k, 1), stage[spot, :])
        return carry

    lax.fori_loop(0, DEV, pack, 0, unroll=8)


def dispatch(vectors, assignment, slot):
    return pl.pallas_call(
        dispatch_kernel,
        out_shape=jax.ShapeDtypeStruct((DEV * BLOCK, LANES), jnp.float32),
        in_specs=[VMEM] * 3,
        out_specs=VMEM,
        scratch_shapes=[
            pltpu.VMEM((TOK, LANES), jnp.float32),
            pltpu.VMEM((DEV * (BLOCK + SEND - MAIN), LANES), jnp.float32),
            pltpu.VMEM((TOK // LANES, LANES), jnp.int32),
            pltpu.SMEM((TOK // LANES, LANES), jnp.int32),
            pltpu.SemaphoreType.DMA,
        ],
        name="dispatch",
    )(vectors, assignment.reshape(TOK // LANES, LANES), slot.reshape(TOK // LANES, LANES))


def place_kernel(got_ref, old_ref, prior_ref, cent_ref, res_ref, stat_ref, energy_ref, cells, tails, lab_v, lab_s, sem):
    f32, i32 = jnp.float32, jnp.int32
    lab_v[...] = got_ref[pl.ds(MAIN, DEV, stride=BLOCK), :].astype(i32)
    copy = pltpu.make_async_copy(lab_v, lab_s, sem)
    copy.start()
    cells[...] = jnp.full(cells.shape, jnp.inf, f32)
    near = lax.broadcasted_iota(i32, (8, LANES), 1)

    def unpack(d, carry):
        first, second, third = (
            pltpu.roll(got_ref[pl.ds(d * BLOCK + 8 * k, 8), :], 32 * k + 32, 1) for k in range(MAIN // 8)
        )
        tail = jnp.where(near < 32, first, jnp.where(near < 64, second, third))
        tails[pl.ds(pl.multiple_of(8 * d, 8), 8), :] = tail
        return carry

    lax.fori_loop(0, DEV, unpack, 0, unroll=8)
    copy.wait()
    for d in range(DEV):
        for r in range(MAIN):
            cells[pl.ds(lab_s[d, r], 1), :] = got_ref[d * BLOCK + r : d * BLOCK + r + 1, :]
        for r in range(MAIN, SEND):
            spot = d * (SEND - MAIN) + r - MAIN
            cells[pl.ds(lab_s[d, r], 1), :] = tails[spot : spot + 1, :]
    lane = lax.broadcasted_iota(i32, (D, LANES), 1)
    to_lane = jnp.bitwise_and(lane, 15) * 8 + lax.shift_right_logical(lane, 4)
    to_list = jnp.bitwise_and(lane, 7) * 16 + lax.shift_right_logical(lane, 3)
    total = jnp.zeros((8, LANES), f32)
    for h in range(LISTS // LANES):
        span = slice(h * LANES, (h + 1) * LANES)
        sums = jnp.zeros((D, LANES), f32)
        counts = jnp.zeros((1, LANES), f32)
        seen = []
        for j in range(CAP):
            start = j * LISTS + h * LANES
            block = cells[start : start + LANES, :].T[:D]
            full = block[:1] < jnp.inf
            block = jnp.where(full, block, 0.0)
            here = jnp.where(full, 1.0, 0.0)
            sums = sums + block
            counts = counts + here
            seen.append(here)
            res_ref[j, :, span] = block
        prior8 = jnp.broadcast_to(prior_ref[:, span].astype(f32), (8, LANES))
        prior = jnp.take_along_axis(prior8, to_lane[:8], axis=1)[:1]
        old = jnp.take_along_axis(old_ref[:, span], to_lane, axis=1)
        weight = prior + counts
        cent = (prior * old + sums) / weight
        cent_ref[:, span] = jnp.take_along_axis(cent, to_list, axis=1)
        stat_ref[:, span] = jnp.concatenate([prior, weight, jnp.zeros((6, LANES), f32)], axis=0)
        for j in range(CAP):
            res = res_ref[j, :, span] - cent * seen[j]
            res_ref[j, :, span] = res
            square = res * res
            for t in range(D // 8):
                total = total + square[8 * t : 8 * t + 8]
    energy_ref[...] = jnp.broadcast_to(jnp.sum(total, axis=0, keepdims=True), (DEV, LANES))


def place(got, old_centroids, prior_counts):
    f32 = jnp.float32
    return pl.pallas_call(
        place_kernel,
        out_shape=(
            jax.ShapeDtypeStruct((D, LISTS), f32),
            jax.ShapeDtypeStruct((CAP, D, LISTS), f32),
            jax.ShapeDtypeStruct((8, LISTS), f32),
            jax.ShapeDtypeStruct((DEV, LANES), f32),
        ),
        in_specs=[VMEM] * 3,
        out_specs=(VMEM,) * 4,
        scratch_shapes=[
            pltpu.VMEM((CELLS + 8, LANES), f32),
            pltpu.VMEM((DEV * (SEND - MAIN), LANES), f32),
            pltpu.VMEM((DEV, LANES), jnp.int32),
            pltpu.SMEM((DEV, LANES), jnp.int32),
            pltpu.SemaphoreType.DMA,
        ],
        name="place",
    )(got, old_centroids, prior_counts.reshape(1, LISTS))


def gram_kernel(res_ref, gram_ref):
    def row(i, carry):
        for h in range(LISTS // LANES):
            span = slice(h * LANES, (h + 1) * LANES)
            left = res_ref[i, :, span]
            for step in range(CAP // 2 + 1):
                j = jnp.bitwise_and(i + step, CAP - 1)
                value = jnp.sum(left * res_ref[j, :, span], axis=0, keepdims=True)
                gram_ref[h, i, pl.ds(j, 1), :] = value
                gram_ref[h, j, pl.ds(i, 1), :] = value
        return carry

    lax.fori_loop(0, CAP, row, 0)


def gram(res):
    return pl.pallas_call(
        gram_kernel,
        out_shape=jax.ShapeDtypeStruct((LISTS // LANES, CAP, CAP, LANES), jnp.float32),
        in_specs=[VMEM],
        out_specs=VMEM,
        cost_estimate=pl.CostEstimate(flops=2 * CAP * CAP * D * LISTS, bytes_accessed=4 * CAP * D * LISTS, transcendentals=0),
        name="gram",
    )(res)


def whiten_kernel(res_ref, gram_ref, stat_ref, energy_ref, out_ref, t_ref, z_ref, s_ref, q_ref, o_ref):
    f32, i32 = jnp.float32, jnp.int32
    group = 4
    row_of = lax.broadcasted_iota(i32, (CAP, LANES), 0)
    energy = jnp.sum(energy_ref[...], axis=(0, 1), keepdims=True)
    shrinkage = shrink_weight * energy / TOTAL + epsilon
    for h in range(LISTS // LANES):
        span = slice(h * LANES, (h + 1) * LANES)
        weight = stat_ref[1:2, span]
        share = 1.0 / weight
        ridge = shrinkage * stat_ref[0:1, span]
        frob = jnp.zeros((CAP, LANES), f32)
        for i in range(CAP):
            row = (gram_ref[h, i] + jnp.where(row_of == i, ridge, 0.0)) * share
            t_ref[i] = row
            frob = frob + row * row
        ridge = ridge * share
        frob = jnp.sqrt(jnp.sum(frob, axis=0, keepdims=True) + TAIL * (ridge * ridge))
        scale = 1.0 / frob
        middle = []
        for i in range(CAP):
            row = t_ref[i] * scale
            t_ref[i] = row
            middle.append(jnp.where(row_of == i, 1.5, 0.0) - 0.5 * row)
            z_ref[i] = middle[i]

        def times(left, i, middle):
            total = left[i, 0:1, :] * middle[0]
            for k in range(1, CAP):
                total = total + left[i, k : k + 1, :] * middle[k]
            return total

        for step in range(STEPS):

            def advance(block, carry, step=step, middle=middle):
                spots = [block * group + g for g in range(group)]
                if step < STEPS - 1:
                    for i in spots:
                        s_ref[i] = times(t_ref, i, middle)
                if step > 0:
                    for i in spots:
                        moved = times(z_ref, i, middle)
                        if step == STEPS - 1:
                            q_ref[h, i] = moved * root
                        else:
                            z_ref[i] = moved
                if step < STEPS - 1:
                    for i in spots:
                        t_ref[i] = times(s_ref, i, middle)
                return carry

            root = 1.0 / jnp.sqrt(frob)
            lax.fori_loop(0, CAP // group, advance, 0)
            if step < STEPS - 1:
                middle = [jnp.where(row_of == i, 1.5, 0.0) - 0.5 * t_ref[i] for i in range(CAP)]

    lane = lax.broadcasted_iota(i32, (8, LANES), 1)
    tiles = D // 8

    def weave(n):
        parts = [o_ref[j] for j in range(CAP)]

        def finish():
            h, t = n // tiles, n % tiles
            for bit in (8, 4, 2, 1):
                low = jnp.bitwise_and(lane, bit) == 0
                for j in range(CAP):
                    if j & bit == 0:
                        one, two = parts[j], parts[j | bit]
                        parts[j] = jnp.where(low, one, pltpu.roll(two, bit, 1))
                        parts[j | bit] = jnp.where(low, pltpu.roll(one, LANES - bit, 1), two)
            for j in range(CAP):
                at = pl.multiple_of(h * (CAP * LANES) + j * LANES, LANES)
                out_ref[pl.ds(pl.multiple_of(t * 8, 8), 8), pl.ds(at, LANES)] = parts[j]

        return finish

    def apply(n, carry):
        finish = weave(jnp.maximum(n - 1, 0))
        h, t = n // tiles, n % tiles
        tile = pl.ds(pl.multiple_of(t * 8, 8), 8)
        span = pl.ds(pl.multiple_of(h * LANES, LANES), LANES)
        pieces = [res_ref[i, tile, span] for i in range(CAP)]
        for j in range(CAP):
            total = pieces[0] * q_ref[h, j, 0:1, :]
            for i in range(1, CAP):
                total = total + pieces[i] * q_ref[h, j, i : i + 1, :]
            o_ref[j] = total
        finish()
        return carry

    last = tiles * (LISTS // LANES)
    lax.fori_loop(0, last, apply, 0)
    weave(last - 1)()


def whiten(res, gram_blocks, stat, energy):
    f32 = jnp.float32
    return pl.pallas_call(
        whiten_kernel,
        out_shape=jax.ShapeDtypeStruct((D, CELLS), f32),
        in_specs=[VMEM] * 4,
        out_specs=VMEM,
        scratch_shapes=[pltpu.VMEM((CAP, CAP, LANES), f32)] * 3
        + [pltpu.VMEM((LISTS // LANES, CAP, CAP, LANES), f32), pltpu.VMEM((CAP, 8, LANES), f32)],
        name="whiten",
    )(res, gram_blocks, stat, energy)


def local(vectors, assignment, slot, old_centroids, prior_counts):
    outgoing = dispatch(vectors, assignment, slot).reshape(DEV, 1, BLOCK * LANES)
    incoming = lax.all_to_all(outgoing, AXES, split_axis=0, concat_axis=0, tiled=True)
    centroids, res, stat, energy = place(incoming.reshape(DEV * BLOCK, LANES), old_centroids, prior_counts)
    shared = lax.all_to_all(energy.reshape(DEV, 1, LANES), AXES, split_axis=0, concat_axis=0, tiled=True)
    rotated = whiten(res, gram(res), stat, shared.reshape(DEV, LANES))
    return (centroids, rotated)


def solution(mesh):
    placed = (
        P(None, AXES),
        P(AXES),
        P(AXES),
        P(None, AXES),
        P(AXES),
    )
    return jax.shard_map(
        local,
        mesh=mesh,
        in_specs=placed,
        out_specs=(P(None, AXES), P(None, AXES)),
        check_vma=False,
    )
```

```python
import jax
import jax.numpy as jnp
from jax import lax
from jax.experimental import pallas as pl
from jax.experimental.pallas import tpu as pltpu
from jax.sharding import PartitionSpec as P

D = 96
CAP = 16
LISTS = 256
CELLS = LISTS * CAP
TOK = 2048
DEV = 128
SEND = 32
STEPS = 4
AXES = ("dp", "owner")
LANES = 128
TAIL = D - CAP
MAIN = 24
BLOCK = MAIN + 1
TOTAL = D * TOK * DEV

shrink_weight = 0.5
epsilon = 1e-05

VMEM = pl.BlockSpec(memory_space=pltpu.VMEM)
GRANT = 16 * 1024 * 1024


def dispatch_kernel(vec_hbm, assign_hbm, slot_hbm, send_ref, vec_ref, assign_ref, slot_ref, rows, stage, pos_v, pos_s, sem):
    f32, bf16, i32 = jnp.float32, jnp.bfloat16, jnp.int32
    wide = 2 * LANES
    get_assign = pltpu.make_async_copy(assign_hbm, assign_ref, sem.at[0])
    get_slot = pltpu.make_async_copy(slot_hbm, slot_ref, sem.at[1])
    get_vectors = pltpu.make_async_copy(vec_hbm, vec_ref, sem.at[2])
    get_assign.start()
    get_slot.start()
    get_vectors.start()
    get_assign.wait()
    get_slot.wait()
    assign = assign_ref[...]
    owner = lax.shift_right_logical(assign, 8)
    here = jnp.bitwise_and(assign, LISTS - 1)
    half = jnp.bitwise_and(here, LANES - 1)
    lane = jnp.bitwise_and(here, LANES) + jnp.bitwise_and(half, 7) * 16 + lax.shift_right_logical(half, 3)
    code = slot_ref[...] * LISTS + lane + 1
    code_high = lax.shift_right_logical(code, 6).astype(f32)
    code_low = jnp.bitwise_and(code, 63).astype(f32)

    def pair(x, c):
        return jnp.concatenate([x[2 * c : 2 * c + 1, :], x[2 * c + 1 : 2 * c + 2, :]], axis=1)

    sub = lax.broadcasted_iota(i32, (LANES, wide), 0)
    slots = lax.broadcasted_iota(i32, (SEND, wide), 0)
    row2 = lax.broadcasted_iota(i32, (wide, wide), 0)
    col2 = lax.broadcasted_iota(i32, (wide, wide), 1)
    before = jnp.concatenate([jnp.where(row2 < col2, 1.0, 0.0), jnp.ones((wide, wide), f32)], axis=1).astype(bf16)
    carry = jnp.zeros((LANES, wide), f32)
    codes = jnp.zeros((LANES, 2 * SEND), f32)
    for c in range(TOK // wide):
        mine = pair(owner, c)
        picked = sub == mine
        hot = jnp.where(picked, 1.0, 0.0).astype(bf16)
        counted = jnp.dot(hot, before, preferred_element_type=f32)
        rank = jnp.sum(jnp.where(picked, counted[:, :wide] + carry, 0.0), axis=0, keepdims=True).astype(i32)
        carry = carry + counted[:, wide:]
        pos = jnp.where(rank < MAIN, mine * BLOCK + rank, DEV * BLOCK - MAIN + mine * (SEND - MAIN) + rank)
        pos_v[2 * c : 2 * c + 1, :] = pos[:, :LANES]
        pos_v[2 * c + 1 : 2 * c + 2, :] = pos[:, LANES:]
        at = slots == rank
        marks = jnp.concatenate(
            [jnp.where(at, pair(code_high, c), 0.0), jnp.where(at, pair(code_low, c), 0.0)], axis=0
        ).astype(bf16)
        codes = codes + lax.dot_general(hot, marks, (((1,), (1,)), ((), ())), preferred_element_type=f32)
    copy = pltpu.make_async_copy(pos_v, pos_s, sem.at[3])
    copy.start()
    labels = codes[:, :SEND] * 64.0 + codes[:, SEND:] - 1.0
    labels = jnp.where(labels < 0.0, float(CELLS), labels)
    labels = jnp.concatenate([labels, jnp.zeros((DEV, LANES - SEND), f32)], axis=1)
    send_ref[pl.ds(MAIN, DEV, stride=BLOCK), :] = labels
    fill = jnp.zeros((LANES - D, LANES), f32)
    get_vectors.wait()
    for c in range(TOK // LANES):
        block = jnp.concatenate([vec_ref[:, c * LANES : (c + 1) * LANES], fill], axis=0)
        rows[c * LANES : (c + 1) * LANES, :] = block.T
    copy.wait()

    def move(t, carry):
        stage[pl.ds(pos_s[t // LANES, t % LANES], 1), :] = rows[pl.ds(t, 1), :]
        return carry

    lax.fori_loop(0, TOK, move, 0, unroll=True)
    outer = lax.broadcasted_iota(i32, (8, LANES), 1) >= D

    def pack(d, carry):
        tail = stage[pl.ds(pl.multiple_of(DEV * BLOCK + 8 * d, 8), 8), :]
        for k in range(MAIN // 8):
            spot = pl.ds(d * BLOCK + 8 * k, 8)
            send_ref[spot, :] = jnp.where(outer, pltpu.roll(tail, D - 32 * k, 1), stage[spot, :])
        return carry

    lax.fori_loop(0, DEV, pack, 0, unroll=8)


def dispatch(vectors, assignment, slot):
    arrays = (vectors, assignment.reshape(TOK // LANES, LANES), slot.reshape(TOK // LANES, LANES))
    return pl.pallas_call(
        dispatch_kernel,
        out_shape=jax.ShapeDtypeStruct((DEV * BLOCK, LANES), jnp.float32),
        in_specs=[pl.BlockSpec(memory_space=pltpu.HBM)] * 3,
        out_specs=VMEM,
        scratch_shapes=[
            pltpu.VMEM((D, TOK), jnp.float32),
            pltpu.VMEM((TOK // LANES, LANES), jnp.int32),
            pltpu.VMEM((TOK // LANES, LANES), jnp.int32),
            pltpu.VMEM((TOK, LANES), jnp.float32),
            pltpu.VMEM((DEV * (BLOCK + SEND - MAIN), LANES), jnp.float32),
            pltpu.VMEM((TOK // LANES, LANES), jnp.int32),
            pltpu.SMEM((TOK // LANES, LANES), jnp.int32),
            pltpu.SemaphoreType.DMA((4,)),
        ],
        compiler_params=pltpu.CompilerParams(vmem_limit_bytes=GRANT),
        name="dispatch",
    )(*(pltpu.with_memory_space_constraint(x, pltpu.HBM) for x in arrays))


def place_kernel(got_ref, old_ref, prior_ref, res_ref, stat_ref, energy_ref, cells, tails, lab_v, lab_s, sem):
    f32, i32 = jnp.float32, jnp.int32
    lab_v[...] = got_ref[pl.ds(MAIN, DEV, stride=BLOCK), :].astype(i32)
    copy = pltpu.make_async_copy(lab_v, lab_s, sem)
    copy.start()
    cells[...] = jnp.full(cells.shape, jnp.inf, f32)
    near = lax.broadcasted_iota(i32, (8, LANES), 1)

    def unpack(d, carry):
        first, second, third = (
            pltpu.roll(got_ref[pl.ds(d * BLOCK + 8 * k, 8), :], 32 * k + 32, 1) for k in range(MAIN // 8)
        )
        tail = jnp.where(near < 32, first, jnp.where(near < 64, second, third))
        tails[pl.ds(pl.multiple_of(8 * d, 8), 8), :] = tail
        return carry

    lax.fori_loop(0, DEV, unpack, 0, unroll=8)
    copy.wait()

    def move(d, carry):
        labels = lab_s.at[d]
        for r in range(MAIN):
            cells[pl.ds(labels[r], 1), :] = got_ref[pl.ds(d * BLOCK + r, 1), :]
        for r in range(MAIN, SEND):
            cells[pl.ds(labels[r], 1), :] = tails[pl.ds(d * (SEND - MAIN) + r - MAIN, 1), :]
        return carry

    lax.fori_loop(0, DEV, move, 0, unroll=True)
    lane = lax.broadcasted_iota(i32, (D, LANES), 1)
    to_lane = jnp.bitwise_and(lane, 15) * 8 + lax.shift_right_logical(lane, 4)
    total = jnp.zeros((8, LANES), f32)
    for h in range(LISTS // LANES):
        span = slice(h * LANES, (h + 1) * LANES)
        sums = jnp.zeros((D, LANES), f32)
        counts = jnp.zeros((1, LANES), f32)
        seen = []
        for j in range(CAP):
            start = j * LISTS + h * LANES
            block = cells[start : start + LANES, :].T[:D]
            full = block[:1] < jnp.inf
            block = jnp.where(full, block, 0.0)
            here = jnp.where(full, 1.0, 0.0)
            sums = sums + block
            counts = counts + here
            seen.append(here)
            res_ref[j, :, span] = block
        prior8 = jnp.broadcast_to(prior_ref[:, span].astype(f32), (8, LANES))
        prior = jnp.take_along_axis(prior8, to_lane[:8], axis=1)[:1]
        old = jnp.take_along_axis(old_ref[:, span], to_lane, axis=1)
        weight = prior + counts
        cent = (prior * old + sums) / weight
        res_ref[CAP, :, span] = cent
        stat_ref[:, span] = jnp.concatenate([prior, weight, jnp.zeros((6, LANES), f32)], axis=0)
        for j in range(CAP):
            res = res_ref[j, :, span] - cent * seen[j]
            res_ref[j, :, span] = res
            square = res * res
            for t in range(D // 8):
                total = total + square[8 * t : 8 * t + 8]
    energy_ref[...] = jnp.broadcast_to(jnp.sum(total, axis=0, keepdims=True), (DEV, LANES))


def place(got, old_centroids, prior_counts):
    f32 = jnp.float32
    return pl.pallas_call(
        place_kernel,
        out_shape=(
            jax.ShapeDtypeStruct((CAP + 1, D, LISTS), f32),
            jax.ShapeDtypeStruct((8, LISTS), f32),
            jax.ShapeDtypeStruct((DEV, LANES), f32),
        ),
        in_specs=[VMEM] * 3,
        out_specs=(VMEM,) * 3,
        scratch_shapes=[
            pltpu.VMEM((CELLS + 8, LANES), f32),
            pltpu.VMEM((DEV * (SEND - MAIN), LANES), f32),
            pltpu.VMEM((DEV, LANES), jnp.int32),
            pltpu.SMEM((DEV, LANES), jnp.int32),
            pltpu.SemaphoreType.DMA,
        ],
        compiler_params=pltpu.CompilerParams(vmem_limit_bytes=GRANT),
        name="place",
    )(got, old_centroids, prior_counts.reshape(1, LISTS))


def weave(parts, lane):
    parts = list(parts)
    for bit in (8, 4, 2, 1):
        low = jnp.bitwise_and(lane, bit) == 0
        for j in range(CAP):
            if j & bit == 0:
                one, two = parts[j], parts[j | bit]
                parts[j] = jnp.where(low, one, pltpu.roll(two, bit, 1))
                parts[j | bit] = jnp.where(low, pltpu.roll(one, LANES - bit, 1), two)
    return parts


def gram_kernel(res_ref, woven_ref, out_ref, gram_ref):
    f32, i32 = jnp.float32, jnp.int32
    lane = lax.broadcasted_iota(i32, (D, LANES), 1)
    to_list = jnp.bitwise_and(lane, 7) * 16 + lax.shift_right_logical(lane, 3)
    for h in range(LISTS // LANES):
        span = slice(h * LANES, (h + 1) * LANES)
        out_ref[:, span] = jnp.take_along_axis(res_ref[CAP, :, span], to_list, axis=1)

    def row(i, carry):
        for h in range(LISTS // LANES):
            span = slice(h * LANES, (h + 1) * LANES)
            left = res_ref[i, :, span]
            for step in range(CAP // 2 + 1):
                j = jnp.bitwise_and(i + step, CAP - 1)
                value = jnp.sum(left * res_ref[j, :, span], axis=0, keepdims=True)
                gram_ref[h, i, pl.ds(j, 1), :] = value
                gram_ref[h, j, pl.ds(i, 1), :] = value
        return carry

    lax.fori_loop(0, CAP, row, 0)

    def spread(t, carry):
        tile = pl.ds(pl.multiple_of(t * 8, 8), 8)
        for h in range(LISTS // LANES):
            span = slice(h * LANES, (h + 1) * LANES)
            parts = weave([res_ref[j, tile, span] for j in range(CAP)], lane[:8])
            for j in range(CAP):
                at = (h * CAP + j) * LANES
                woven_ref[tile, at : at + LANES] = parts[j]
        return carry

    lax.fori_loop(0, D // 8, spread, 0)
    for h in range(LISTS // LANES):
        for i in range(CAP):
            at = (h * CAP + i) * LANES
            woven_ref[D:, at : at + LANES] = gram_ref[h, i]


def gram(res):
    f32 = jnp.float32
    return pl.pallas_call(
        gram_kernel,
        out_shape=(
            jax.ShapeDtypeStruct((D + CAP, CELLS), f32),
            jax.ShapeDtypeStruct((D, LISTS), f32),
        ),
        in_specs=[VMEM],
        out_specs=(VMEM,) * 2,
        scratch_shapes=[pltpu.VMEM((LISTS // LANES, CAP, CAP, LANES), f32)],
        cost_estimate=pl.CostEstimate(flops=2 * CAP * CAP * D * LISTS, bytes_accessed=8 * CAP * D * LISTS, transcendentals=0),
        compiler_params=pltpu.CompilerParams(vmem_limit_bytes=GRANT),
        name="gram",
    )(res)


def whiten_kernel(woven_ref, stat_ref, energy_ref, out_hbm, t_ref, z_ref, s_ref, q_ref, w_ref, out_ref, sem):
    f32, bf16, i32 = jnp.float32, jnp.bfloat16, jnp.int32
    group = 4
    row_of = lax.broadcasted_iota(i32, (CAP, LANES), 0)
    energy = jnp.sum(energy_ref[...], axis=(0, 1), keepdims=True)
    shrinkage = shrink_weight * energy / TOTAL + epsilon
    for h in range(LISTS // LANES):
        span = slice(h * LANES, (h + 1) * LANES)
        weight = stat_ref[1:2, span]
        share = 1.0 / weight
        ridge = shrinkage * stat_ref[0:1, span]
        frob = jnp.zeros((CAP, LANES), f32)
        for i in range(CAP):
            at = (h * CAP + i) * LANES
            row = (woven_ref[D:, at : at + LANES] + jnp.where(row_of == i, ridge, 0.0)) * share
            t_ref[i] = row
            frob = frob + row * row
        ridge = ridge * share
        frob = jnp.sqrt(jnp.sum(frob, axis=0, keepdims=True) + TAIL * (ridge * ridge))
        scale = 1.0 / frob
        middle = []
        for i in range(CAP):
            row = t_ref[i] * scale
            t_ref[i] = row
            middle.append(jnp.where(row_of == i, 1.5, 0.0) - 0.5 * row)
            z_ref[i] = middle[i]

        def times(left, i, middle):
            total = left[i, 0:1, :] * middle[0]
            for k in range(1, CAP):
                total = total + left[i, k : k + 1, :] * middle[k]
            return total

        for step in range(STEPS):

            def advance(block, carry, step=step, middle=middle):
                spots = [block * group + g for g in range(group)]
                if step < STEPS - 1:
                    for i in spots:
                        s_ref[i] = times(t_ref, i, middle)
                if step > 0:
                    for i in spots:
                        moved = times(z_ref, i, middle)
                        if step == STEPS - 1:
                            q_ref[h, i] = moved * root
                        else:
                            z_ref[i] = moved
                if step < STEPS - 1:
                    for i in spots:
                        t_ref[i] = times(s_ref, i, middle)
                return carry

            root = 1.0 / jnp.sqrt(frob)
            lax.fori_loop(0, CAP // group, advance, 0)
            if step < STEPS - 1:
                middle = [jnp.where(row_of == i, 1.5, 0.0) - 0.5 * t_ref[i] for i in range(CAP)]

    lane = lax.broadcasted_iota(i32, (CAP, LANES), 1)
    for h in range(LISTS // LANES):
        for j, part in enumerate(weave([q_ref[h, i] for i in range(CAP)], lane)):
            w_ref[h * CAP + j] = part
    wide = 2 * LANES
    block = lax.broadcasted_iota(i32, (LANES, LANES), 0) // CAP == lax.broadcasted_iota(i32, (LANES, LANES), 1) // CAP
    empty = jnp.zeros((LANES, LANES), bf16)

    def diagonal(first, second):
        first, second = (
            jnp.where(block, jnp.concatenate([x] * (LANES // CAP), axis=0), 0.0).astype(bf16) for x in (first, second)
        )
        return jnp.concatenate(
            [jnp.concatenate([first, empty], axis=1), jnp.concatenate([empty, second], axis=1)], axis=0
        )

    copies = []
    for g in range(CELLS // wide):
        span = slice(g * wide, (g + 1) * wide)
        pair = [w_ref[2 * g], w_ref[2 * g + 1]]
        coarse = [x.astype(bf16).astype(f32) for x in pair]
        fine = [x - y for x, y in zip(pair, coarse)]
        coarse, fine = diagonal(*coarse), diagonal(*fine)
        value = woven_ref[:D, span]
        high = value.astype(bf16)
        low = (value - high.astype(f32)).astype(bf16)
        out_ref[:, span] = (
            jnp.dot(high, coarse, preferred_element_type=f32)
            + jnp.dot(low, coarse, preferred_element_type=f32)
            + jnp.dot(high, fine, preferred_element_type=f32)
        )
        copies.append(pltpu.make_async_copy(out_ref.at[:, span], out_hbm.at[:, span], sem.at[g]))
        copies[g].start()
    for copy in copies:
        copy.wait()


def whiten(woven, stat, energy):
    f32 = jnp.float32
    return pl.pallas_call(
        whiten_kernel,
        out_shape=jax.ShapeDtypeStruct((D, CELLS), f32),
        in_specs=[VMEM] * 3,
        out_specs=pl.BlockSpec(memory_space=pltpu.HBM),
        scratch_shapes=[pltpu.VMEM((CAP, CAP, LANES), f32)] * 3
        + [
            pltpu.VMEM((LISTS // LANES, CAP, CAP, LANES), f32),
            pltpu.VMEM((CELLS // LANES, CAP, LANES), f32),
            pltpu.VMEM((D, CELLS), f32),
            pltpu.SemaphoreType.DMA((CELLS // (2 * LANES),)),
        ],
        compiler_params=pltpu.CompilerParams(vmem_limit_bytes=GRANT),
        name="whiten",
    )(woven, stat, energy)


def local(vectors, assignment, slot, old_centroids, prior_counts):
    outgoing = dispatch(vectors, assignment, slot).reshape(DEV, 1, BLOCK * LANES)
    incoming = lax.all_to_all(outgoing, AXES, split_axis=0, concat_axis=0, tiled=True)
    res, stat, energy = place(incoming.reshape(DEV * BLOCK, LANES), old_centroids, prior_counts)
    shared = lax.all_to_all(energy.reshape(DEV, 1, LANES), AXES, split_axis=0, concat_axis=0, tiled=True)
    woven, centroids = gram(res)
    rotated = whiten(woven, stat, shared.reshape(DEV, LANES))
    return (centroids, rotated)


def solution(mesh):
    placed = (
        P(None, AXES),
        P(AXES),
        P(AXES),
        P(None, AXES),
        P(AXES),
    )
    return jax.shard_map(
        local,
        mesh=mesh,
        in_specs=placed,
        out_specs=(P(None, AXES), P(None, AXES)),
        check_vma=False,
    )
```

```python
import jax
import jax.numpy as jnp
from jax import lax
from jax.experimental import pallas as pl
from jax.experimental.pallas import tpu as pltpu
from jax.sharding import PartitionSpec as P

D = 96
CAP = 16
LISTS = 256
CELLS = LISTS * CAP
TOK = 2048
DEV = 128
SEND = 32
STEPS = 4
AXES = ("dp", "owner")
LANES = 128
TAIL = D - CAP
MAIN = 24
BLOCK = MAIN + 1
POWERS = 4
TOTAL = D * TOK * DEV

shrink_weight = 0.5
epsilon = 1e-05

VMEM = pl.BlockSpec(memory_space=pltpu.VMEM)
HBM = pl.BlockSpec(memory_space=pltpu.HBM)
GRANT = 16 * 1024 * 1024


def dispatch_kernel(vec_hbm, assign_hbm, slot_hbm, send_ref, vec_ref, assign_ref, slot_ref, rows, stage, pos_v, pos_s, sem):
    f32, bf16, i32 = jnp.float32, jnp.bfloat16, jnp.int32
    wide = 2 * LANES
    get_assign = pltpu.make_async_copy(assign_hbm, assign_ref, sem.at[0])
    get_slot = pltpu.make_async_copy(slot_hbm, slot_ref, sem.at[1])
    get_vectors = pltpu.make_async_copy(vec_hbm, vec_ref, sem.at[2])
    get_assign.start()
    get_slot.start()
    get_vectors.start()
    get_assign.wait()
    get_slot.wait()
    assign = assign_ref[...]
    owner = lax.shift_right_logical(assign, 8)
    here = jnp.bitwise_and(assign, LISTS - 1)
    half = jnp.bitwise_and(here, LANES - 1)
    lane = jnp.bitwise_and(here, LANES) + jnp.bitwise_and(half, 7) * 16 + lax.shift_right_logical(half, 3)
    code = slot_ref[...] * LISTS + lane + 1
    code_high = lax.shift_right_logical(code, 6).astype(f32)
    code_low = jnp.bitwise_and(code, 63).astype(f32)

    def pair(x, c):
        return jnp.concatenate([x[2 * c : 2 * c + 1, :], x[2 * c + 1 : 2 * c + 2, :]], axis=1)

    sub = lax.broadcasted_iota(i32, (LANES, wide), 0)
    slots = lax.broadcasted_iota(i32, (SEND, wide), 0)
    row2 = lax.broadcasted_iota(i32, (wide, wide), 0)
    col2 = lax.broadcasted_iota(i32, (wide, wide), 1)
    before = jnp.concatenate([jnp.where(row2 < col2, 1.0, 0.0), jnp.ones((wide, wide), f32)], axis=1).astype(bf16)
    carry = jnp.zeros((LANES, wide), f32)
    codes = jnp.zeros((LANES, 2 * SEND), f32)
    for c in range(TOK // wide):
        mine = pair(owner, c)
        picked = sub == mine
        hot = jnp.where(picked, 1.0, 0.0).astype(bf16)
        counted = jnp.dot(hot, before, preferred_element_type=f32)
        rank = jnp.sum(jnp.where(picked, counted[:, :wide] + carry, 0.0), axis=0, keepdims=True).astype(i32)
        carry = carry + counted[:, wide:]
        pos = jnp.where(rank < MAIN, mine * BLOCK + rank, DEV * BLOCK - MAIN + mine * (SEND - MAIN) + rank)
        pos_v[2 * c : 2 * c + 1, :] = pos[:, :LANES]
        pos_v[2 * c + 1 : 2 * c + 2, :] = pos[:, LANES:]
        at = slots == rank
        marks = jnp.concatenate(
            [jnp.where(at, pair(code_high, c), 0.0), jnp.where(at, pair(code_low, c), 0.0)], axis=0
        ).astype(bf16)
        codes = codes + lax.dot_general(hot, marks, (((1,), (1,)), ((), ())), preferred_element_type=f32)
    copy = pltpu.make_async_copy(pos_v, pos_s, sem.at[3])
    copy.start()
    labels = codes[:, :SEND] * 64.0 + codes[:, SEND:] - 1.0
    labels = jnp.where(labels < 0.0, float(CELLS), labels)
    labels = jnp.concatenate([labels, jnp.zeros((DEV, LANES - SEND), f32)], axis=1)
    send_ref[pl.ds(MAIN, DEV, stride=BLOCK), :] = labels
    fill = jnp.zeros((LANES - D, LANES), f32)
    get_vectors.wait()
    for c in range(TOK // LANES):
        block = jnp.concatenate([vec_ref[:, c * LANES : (c + 1) * LANES], fill], axis=0)
        rows[c * LANES : (c + 1) * LANES, :] = block.T
    copy.wait()

    def move(t, carry):
        stage[pl.ds(pos_s[t // LANES, t % LANES], 1), :] = rows[pl.ds(t, 1), :]
        return carry

    lax.fori_loop(0, TOK, move, 0, unroll=True)
    outer = lax.broadcasted_iota(i32, (8, LANES), 1) >= D

    def pack(d, carry):
        tail = stage[pl.ds(pl.multiple_of(DEV * BLOCK + 8 * d, 8), 8), :]
        for k in range(MAIN // 8):
            spot = pl.ds(d * BLOCK + 8 * k, 8)
            send_ref[spot, :] = jnp.where(outer, pltpu.roll(tail, D - 32 * k, 1), stage[spot, :])
        return carry

    lax.fori_loop(0, DEV, pack, 0, unroll=8)


def dispatch(vectors, assignment, slot):
    arrays = (vectors, assignment.reshape(TOK // LANES, LANES), slot.reshape(TOK // LANES, LANES))
    return pl.pallas_call(
        dispatch_kernel,
        out_shape=jax.ShapeDtypeStruct((DEV * BLOCK, LANES), jnp.float32),
        in_specs=[pl.BlockSpec(memory_space=pltpu.HBM)] * 3,
        out_specs=VMEM,
        scratch_shapes=[
            pltpu.VMEM((D, TOK), jnp.float32),
            pltpu.VMEM((TOK // LANES, LANES), jnp.int32),
            pltpu.VMEM((TOK // LANES, LANES), jnp.int32),
            pltpu.VMEM((TOK, LANES), jnp.float32),
            pltpu.VMEM((DEV * (BLOCK + SEND - MAIN), LANES), jnp.float32),
            pltpu.VMEM((TOK // LANES, LANES), jnp.int32),
            pltpu.SMEM((TOK // LANES, LANES), jnp.int32),
            pltpu.SemaphoreType.DMA((4,)),
        ],
        compiler_params=pltpu.CompilerParams(vmem_limit_bytes=GRANT),
        name="dispatch",
    )(*(pltpu.with_memory_space_constraint(x, pltpu.HBM) for x in arrays))


def place_kernel(got_ref, old_ref, prior_ref, res_hbm, stat_ref, energy_ref, res_ref, cells, tails, lab_v, lab_s, sem, out_sem):
    f32, i32 = jnp.float32, jnp.int32
    lab_v[...] = got_ref[pl.ds(MAIN, DEV, stride=BLOCK), :].astype(i32)
    copy = pltpu.make_async_copy(lab_v, lab_s, sem)
    copy.start()
    cells[...] = jnp.full(cells.shape, jnp.inf, f32)
    near = lax.broadcasted_iota(i32, (8, LANES), 1)

    def unpack(d, carry):
        first, second, third = (
            pltpu.roll(got_ref[pl.ds(d * BLOCK + 8 * k, 8), :], 32 * k + 32, 1) for k in range(MAIN // 8)
        )
        tail = jnp.where(near < 32, first, jnp.where(near < 64, second, third))
        tails[pl.ds(pl.multiple_of(d * (SEND - MAIN), 8), 8), :] = tail
        return carry

    lax.fori_loop(0, DEV, unpack, 0, unroll=8)
    copy.wait()

    def move(d, carry):
        for r in range(MAIN):
            cells[pl.ds(lab_s[d, r], 1), :] = got_ref[pl.ds(d * BLOCK + r, 1), :]
        for r in range(MAIN, SEND):
            cells[pl.ds(lab_s[d, r], 1), :] = tails[pl.ds(d * (SEND - MAIN) + r - MAIN, 1), :]
        return carry

    lax.fori_loop(0, DEV, move, 0, unroll=True)
    lane = lax.broadcasted_iota(i32, (D, LANES), 1)
    to_lane = jnp.bitwise_and(lane, 15) * 8 + lax.shift_right_logical(lane, 4)
    total = jnp.zeros((8, LANES), f32)
    outs = []
    for h in range(LISTS // LANES):
        span = slice(h * LANES, (h + 1) * LANES)
        sums = jnp.zeros((D, LANES), f32)
        counts = jnp.zeros((1, LANES), f32)
        seen = []
        for j in range(CAP):
            start = j * LISTS + h * LANES
            block = cells[start : start + LANES, :].T[:D]
            full = block[:1] < jnp.inf
            block = jnp.where(full, block, 0.0)
            here = jnp.where(full, 1.0, 0.0)
            sums = sums + block
            counts = counts + here
            seen.append(here)
            res_ref[j, :, span] = block
        prior8 = jnp.broadcast_to(prior_ref[:, span].astype(f32), (8, LANES))
        prior = jnp.take_along_axis(prior8, to_lane[:8], axis=1)[:1]
        old = jnp.take_along_axis(old_ref[:, span], to_lane, axis=1)
        weight = prior + counts
        cent = (prior * old + sums) / weight
        res_ref[CAP, :, span] = cent
        stat_ref[:, span] = jnp.concatenate([prior, weight, jnp.zeros((6, LANES), f32)], axis=0)
        for j in range(CAP):
            res = res_ref[j, :, span] - cent * seen[j]
            res_ref[j, :, span] = res
            square = res * res
            for t in range(D // 8):
                total = total + square[8 * t : 8 * t + 8]
        outs.append(pltpu.make_async_copy(res_ref.at[:, :, span], res_hbm.at[:, :, span], out_sem.at[h]))
        outs[h].start()
    energy_ref[...] = jnp.broadcast_to(jnp.sum(total, axis=0, keepdims=True), (DEV, LANES))
    for out in outs:
        out.wait()


def place(got, old_centroids, prior_counts):
    f32 = jnp.float32
    return pl.pallas_call(
        place_kernel,
        out_shape=(
            pltpu.HBM((CAP + 1, D, LISTS), f32),
            jax.ShapeDtypeStruct((8, LISTS), f32),
            jax.ShapeDtypeStruct((DEV, LANES), f32),
        ),
        in_specs=[VMEM] * 3,
        out_specs=(HBM, VMEM, VMEM),
        scratch_shapes=[
            pltpu.VMEM((CAP + 1, D, LISTS), f32),
            pltpu.VMEM((CELLS + 8, LANES), f32),
            pltpu.VMEM((DEV * (SEND - MAIN), LANES), f32),
            pltpu.VMEM((DEV, LANES), jnp.int32),
            pltpu.SMEM((DEV, LANES), jnp.int32),
            pltpu.SemaphoreType.DMA,
            pltpu.SemaphoreType.DMA((LISTS // LANES,)),
        ],
        compiler_params=pltpu.CompilerParams(vmem_limit_bytes=GRANT),
        name="place",
    )(got, old_centroids, prior_counts.reshape(1, LISTS))


def weave(parts, lane):
    parts = list(parts)
    for bit in (8, 4, 2, 1):
        low = jnp.bitwise_and(lane, bit) == 0
        for j in range(CAP):
            if j & bit == 0:
                one, two = parts[j], parts[j | bit]
                parts[j] = jnp.where(low, one, pltpu.roll(two, bit, 1))
                parts[j | bit] = jnp.where(low, pltpu.roll(one, LANES - bit, 1), two)
    return parts


def times(left, i, right):
    total = left[i, 0:1, :] * right[0]
    for k in range(1, CAP):
        total = total + left[i, k : k + 1, :] * right[k]
    return total


def gram_kernel(res_hbm, woven_ref, out_ref, gram_ref, next_ref, res_ref, sem):
    f32, i32 = jnp.float32, jnp.int32
    get = pltpu.make_async_copy(res_hbm, res_ref, sem)
    get.start()
    get.wait()
    lane = lax.broadcasted_iota(i32, (D, LANES), 1)
    to_list = jnp.bitwise_and(lane, 7) * 16 + lax.shift_right_logical(lane, 3)
    for h in range(LISTS // LANES):
        span = slice(h * LANES, (h + 1) * LANES)
        out_ref[:, span] = jnp.take_along_axis(res_ref[CAP, :, span], to_list, axis=1)

    def row(i, carry):
        for h in range(LISTS // LANES):
            span = slice(h * LANES, (h + 1) * LANES)
            left = res_ref[i, :, span]
            for step in range(CAP // 2 + 1):
                j = jnp.bitwise_and(i + step, CAP - 1)
                value = jnp.sum(left * res_ref[j, :, span], axis=0, keepdims=True)
                gram_ref[h, i, pl.ds(j, 1), :] = value
                gram_ref[h, j, pl.ds(i, 1), :] = value
        return carry

    lax.fori_loop(0, CAP, row, 0)

    def spread(t, carry):
        tile = pl.ds(pl.multiple_of(t * 8, 8), 8)
        for h in range(LISTS // LANES):
            span = slice(h * LANES, (h + 1) * LANES)
            parts = weave([res_ref[j, tile, span] for j in range(CAP)], lane[:8])
            for j in range(CAP):
                at = (h * CAP + j) * LANES
                woven_ref[tile, at : at + LANES] = parts[j]
        return carry

    lax.fori_loop(0, D // 8, spread, 0)
    group = 4
    for h in range(LISTS // LANES):
        trace = gram_ref[h, 0, 0:1, :]
        for i in range(1, CAP):
            trace = trace + gram_ref[h, i, i : i + 1, :]
        trace = jnp.where(trace > 0.0, trace, 1.0)
        woven_ref[D + POWERS * CAP :, h * LANES : (h + 1) * LANES] = jnp.broadcast_to(trace, (8, LANES))
        unit = 1.0 / trace
        base = []
        for i in range(CAP):
            row = gram_ref[h, i] * unit
            base.append(row)
            next_ref[0, i] = row
            at = (h * CAP + i) * LANES
            woven_ref[D : D + CAP, at : at + LANES] = row

        def raise_rows(block, carry, h=h, base=base):
            spots = [block * group + g for g in range(group)]
            for power in range(1, POWERS):
                for i in spots:
                    row = times(next_ref.at[power - 1], i, base)
                    if power < POWERS - 1:
                        next_ref[power, i] = row
                    at = pl.multiple_of((h * CAP + i) * LANES, LANES)
                    woven_ref[D + power * CAP : D + (power + 1) * CAP, pl.ds(at, LANES)] = row
            return carry

        lax.fori_loop(0, CAP // group, raise_rows, 0)


def gram(res):
    f32 = jnp.float32
    return pl.pallas_call(
        gram_kernel,
        out_shape=(
            jax.ShapeDtypeStruct((D + POWERS * CAP + 8, CELLS), f32),
            jax.ShapeDtypeStruct((D, LISTS), f32),
        ),
        in_specs=[HBM],
        out_specs=(VMEM,) * 2,
        scratch_shapes=[
            pltpu.VMEM((LISTS // LANES, CAP, CAP, LANES), f32),
            pltpu.VMEM((POWERS - 1, CAP, CAP, LANES), f32),
            pltpu.VMEM((CAP + 1, D, LISTS), f32),
            pltpu.SemaphoreType.DMA,
        ],
        cost_estimate=pl.CostEstimate(flops=2 * CAP * CAP * D * LISTS, bytes_accessed=8 * CAP * D * LISTS, transcendentals=0),
        compiler_params=pltpu.CompilerParams(vmem_limit_bytes=GRANT),
        name="gram",
    )(pltpu.with_memory_space_constraint(res, pltpu.HBM))


def whiten_kernel(woven_ref, stat_ref, energy_ref, out_hbm, t_ref, z_ref, s_ref, q_ref, w_ref, out_ref, sem):
    f32, bf16, i32 = jnp.float32, jnp.bfloat16, jnp.int32
    group = 4
    row_of = lax.broadcasted_iota(i32, (CAP, LANES), 0)
    energy = jnp.sum(energy_ref[...], axis=(0, 1), keepdims=True)
    shrinkage = shrink_weight * energy / TOTAL + epsilon
    for h in range(LISTS // LANES):
        span = slice(h * LANES, (h + 1) * LANES)
        prior, weight = stat_ref[0:1, span], stat_ref[1:2, span]
        trace = woven_ref[D + POWERS * CAP : D + POWERS * CAP + 1, span]
        share = 1.0 / weight
        ridge = shrinkage * prior * share
        trace = trace * share

        def power(k, i):
            at = (h * CAP + i) * LANES
            return woven_ref[D + k * CAP : D + (k + 1) * CAP, at : at + LANES]

        frob = jnp.zeros((CAP, LANES), f32)
        for i in range(CAP):
            row = trace * power(0, i) + jnp.where(row_of == i, ridge, 0.0)
            frob = frob + row * row
        frob = jnp.sqrt(jnp.sum(frob, axis=0, keepdims=True) + TAIL * (ridge * ridge))
        scale = 1.0 / frob
        a, x = trace * scale, ridge * scale
        t0 = x * (2.25 + x * (0.25 * x - 1.5))
        t1 = a * (2.25 + x * (0.75 * x - 3.0))
        t2 = a * a * (0.75 * x - 1.5)
        t3 = a * a * a * 0.25
        z0 = 2.25 + x * (-2.4375 + x * (1.6875 + x * (0.0625 * x - 0.5625)))
        z1 = a * (-2.4375 + x * (3.375 + x * (0.25 * x - 1.6875)))
        z2 = a * a * (1.6875 + x * (0.375 * x - 1.6875))
        z3 = a * a * a * (0.25 * x - 0.5625)
        z4 = a * a * (a * a) * 0.0625
        middle = []
        for i in range(CAP):
            own = row_of == i
            h1, h2, h3, h4 = (power(k, i) for k in range(POWERS))
            row = t1 * h1 + t2 * h2 + t3 * h3 + jnp.where(own, t0, 0.0)
            t_ref[i] = row
            z_ref[i] = z1 * h1 + z2 * h2 + z3 * h3 + z4 * h4 + jnp.where(own, z0, 0.0)
            middle.append(jnp.where(own, 1.5, 0.0) - 0.5 * row)
        root = 1.0 / jnp.sqrt(frob)

        for step in range(1, STEPS):

            def advance(block, carry, step=step, middle=middle, root=root, h=h):
                spots = [block * group + g for g in range(group)]
                if step < STEPS - 1:
                    for i in spots:
                        s_ref[i] = times(t_ref, i, middle)
                if step > 1:
                    for i in spots:
                        moved = times(z_ref, i, middle)
                        if step == STEPS - 1:
                            q_ref[h, i] = moved * root
                        else:
                            z_ref[i] = moved
                if step < STEPS - 1:
                    for i in spots:
                        t_ref[i] = times(s_ref, i, middle)
                return carry

            lax.fori_loop(0, CAP // group, advance, 0)
            if step < STEPS - 1:
                middle = [jnp.where(row_of == i, 1.5, 0.0) - 0.5 * t_ref[i] for i in range(CAP)]

    lane = lax.broadcasted_iota(i32, (CAP, LANES), 1)
    for h in range(LISTS // LANES):
        for j, part in enumerate(weave([q_ref[h, i] for i in range(CAP)], lane)):
            w_ref[h * CAP + j] = part
    wide = 2 * LANES
    block = lax.broadcasted_iota(i32, (LANES, LANES), 0) // CAP == lax.broadcasted_iota(i32, (LANES, LANES), 1) // CAP
    empty = jnp.zeros((LANES, LANES), bf16)

    def diagonal(first, second):
        first, second = (
            jnp.where(block, jnp.concatenate([x] * (LANES // CAP), axis=0), 0.0).astype(bf16) for x in (first, second)
        )
        return jnp.concatenate(
            [jnp.concatenate([first, empty], axis=1), jnp.concatenate([empty, second], axis=1)], axis=0
        )

    copies = []
    for g in range(CELLS // wide):
        span = slice(g * wide, (g + 1) * wide)
        pair = [w_ref[2 * g], w_ref[2 * g + 1]]
        coarse = [x.astype(bf16).astype(f32) for x in pair]
        fine = [x - y for x, y in zip(pair, coarse)]
        coarse, fine = diagonal(*coarse), diagonal(*fine)
        value = woven_ref[:D, span]
        high = value.astype(bf16)
        low = (value - high.astype(f32)).astype(bf16)
        out_ref[:, span] = (
            jnp.dot(high, coarse, preferred_element_type=f32)
            + jnp.dot(low, coarse, preferred_element_type=f32)
            + jnp.dot(high, fine, preferred_element_type=f32)
        )
        copies.append(pltpu.make_async_copy(out_ref.at[:, span], out_hbm.at[:, span], sem.at[g]))
        copies[g].start()
    for copy in copies:
        copy.wait()


def whiten(woven, stat, energy):
    f32 = jnp.float32
    return pl.pallas_call(
        whiten_kernel,
        out_shape=jax.ShapeDtypeStruct((D, CELLS), f32),
        in_specs=[VMEM] * 3,
        out_specs=pl.BlockSpec(memory_space=pltpu.HBM),
        scratch_shapes=[pltpu.VMEM((CAP, CAP, LANES), f32)] * 3
        + [
            pltpu.VMEM((LISTS // LANES, CAP, CAP, LANES), f32),
            pltpu.VMEM((CELLS // LANES, CAP, LANES), f32),
            pltpu.VMEM((D, CELLS), f32),
            pltpu.SemaphoreType.DMA((CELLS // (2 * LANES),)),
        ],
        compiler_params=pltpu.CompilerParams(vmem_limit_bytes=GRANT),
        name="whiten",
    )(woven, stat, energy)


def local(vectors, assignment, slot, old_centroids, prior_counts):
    outgoing = dispatch(vectors, assignment, slot).reshape(DEV, 1, BLOCK * LANES)
    incoming = lax.all_to_all(outgoing, AXES, split_axis=0, concat_axis=0, tiled=True)
    res, stat, energy = place(incoming.reshape(DEV * BLOCK, LANES), old_centroids, prior_counts)
    shared = lax.all_to_all(energy.reshape(DEV, 1, LANES), AXES, split_axis=0, concat_axis=0, tiled=True)
    woven, centroids = gram(res)
    rotated = whiten(woven, stat, shared.reshape(DEV, LANES))
    return (centroids, rotated)


def solution(mesh):
    placed = (
        P(None, AXES),
        P(AXES),
        P(AXES),
        P(None, AXES),
        P(AXES),
    )
    return jax.shard_map(
        local,
        mesh=mesh,
        in_specs=placed,
        out_specs=(P(None, AXES), P(None, AXES)),
        check_vma=False,
    )
```

```python
import jax
import jax.numpy as jnp
from jax import lax
from jax.experimental import pallas as pl
from jax.experimental.pallas import tpu as pltpu
from jax.sharding import PartitionSpec as P

D = 96
CAP = 16
LISTS = 256
CELLS = LISTS * CAP
TOK = 2048
DEV = 128
SEND = 32
STEPS = 4
AXES = ("dp", "owner")
LANES = 128
TAIL = D - CAP
MAIN = 24
BLOCK = MAIN + 1
POWERS = 4
TOTAL = D * TOK * DEV

shrink_weight = 0.5
epsilon = 1e-05

VMEM = pl.BlockSpec(memory_space=pltpu.VMEM)
HBM = pl.BlockSpec(memory_space=pltpu.HBM)
GRANT = 16 * 1024 * 1024


def dispatch_kernel(vec_hbm, assign_hbm, slot_hbm, send_ref, vec_ref, assign_ref, slot_ref, rows, stage, pos_v, pos_s, sem):
    f32, bf16, i32 = jnp.float32, jnp.bfloat16, jnp.int32
    wide = 2 * LANES
    get_assign = pltpu.make_async_copy(assign_hbm, assign_ref, sem.at[0])
    get_slot = pltpu.make_async_copy(slot_hbm, slot_ref, sem.at[1])
    get_vectors = pltpu.make_async_copy(vec_hbm, vec_ref, sem.at[2])
    get_assign.start()
    get_slot.start()
    get_vectors.start()
    get_assign.wait()
    get_slot.wait()
    assign = assign_ref[...]
    owner = lax.shift_right_logical(assign, 8)
    here = jnp.bitwise_and(assign, LISTS - 1)
    half = jnp.bitwise_and(here, LANES - 1)
    lane = jnp.bitwise_and(here, LANES) + jnp.bitwise_and(half, 7) * 16 + lax.shift_right_logical(half, 3)
    code = slot_ref[...] * LISTS + lane + 1
    code_high = lax.shift_right_logical(code, 6).astype(f32)
    code_low = jnp.bitwise_and(code, 63).astype(f32)

    def pair(x, c):
        return jnp.concatenate([x[2 * c : 2 * c + 1, :], x[2 * c + 1 : 2 * c + 2, :]], axis=1)

    sub = lax.broadcasted_iota(i32, (LANES, wide), 0)
    slots = lax.broadcasted_iota(i32, (SEND, wide), 0)
    row2 = lax.broadcasted_iota(i32, (wide, wide), 0)
    col2 = lax.broadcasted_iota(i32, (wide, wide), 1)
    before = jnp.concatenate([jnp.where(row2 < col2, 1.0, 0.0), jnp.ones((wide, wide), f32)], axis=1).astype(bf16)
    picks = [sub == pair(owner, c) for c in range(TOK // wide)]
    hots = [jnp.where(x, 1.0, 0.0).astype(bf16) for x in picks]
    counts = jnp.dot(jnp.concatenate(hots, axis=0), before, preferred_element_type=f32)
    carry = jnp.zeros((LANES, wide), f32)
    codes = jnp.zeros((LANES, 2 * SEND), f32)
    for c in range(TOK // wide):
        mine = pair(owner, c)
        picked, hot = picks[c], hots[c]
        counted = counts[c * LANES : (c + 1) * LANES]
        rank = jnp.sum(jnp.where(picked, counted[:, :wide] + carry, 0.0), axis=0, keepdims=True).astype(i32)
        carry = carry + counted[:, wide:]
        pos = jnp.where(rank < MAIN, mine * BLOCK + rank, DEV * BLOCK - MAIN + mine * (SEND - MAIN) + rank)
        pos_v[2 * c : 2 * c + 1, :] = pos[:, :LANES]
        pos_v[2 * c + 1 : 2 * c + 2, :] = pos[:, LANES:]
        at = slots == rank
        marks = jnp.concatenate(
            [jnp.where(at, pair(code_high, c), 0.0), jnp.where(at, pair(code_low, c), 0.0)], axis=0
        ).astype(bf16)
        codes = codes + lax.dot_general(hot, marks, (((1,), (1,)), ((), ())), preferred_element_type=f32)
    copy = pltpu.make_async_copy(pos_v, pos_s, sem.at[3])
    copy.start()
    labels = codes[:, :SEND] * 64.0 + codes[:, SEND:] - 1.0
    labels = jnp.where(labels < 0.0, float(CELLS), labels)
    labels = jnp.concatenate([labels, jnp.zeros((DEV, LANES - SEND), f32)], axis=1)
    send_ref[pl.ds(MAIN, DEV, stride=BLOCK), :] = labels
    get_vectors.wait()
    for c in range(TOK // LANES):
        block = vec_ref[:, c * LANES : (c + 1) * LANES]
        block = jnp.concatenate([block, block[: LANES - D]], axis=0)
        rows[c * LANES : (c + 1) * LANES, :] = block.T
    copy.wait()

    def move(t, carry):
        stage[pl.ds(pos_s[t // LANES, t % LANES], 1), :] = rows[pl.ds(t, 1), :]
        return carry

    lax.fori_loop(0, TOK, move, 0, unroll=True)
    outer = lax.broadcasted_iota(i32, (8, LANES), 1) >= D

    def pack(d, carry):
        tail = stage[pl.ds(pl.multiple_of(DEV * BLOCK + 8 * d, 8), 8), :]
        for k in range(MAIN // 8):
            spot = pl.ds(d * BLOCK + 8 * k, 8)
            send_ref[spot, :] = jnp.where(outer, pltpu.roll(tail, D - 32 * k, 1) if k else tail, stage[spot, :])
        return carry

    lax.fori_loop(0, DEV, pack, 0, unroll=8)


def dispatch(vectors, assignment, slot):
    arrays = (vectors, assignment.reshape(TOK // LANES, LANES), slot.reshape(TOK // LANES, LANES))
    return pl.pallas_call(
        dispatch_kernel,
        out_shape=jax.ShapeDtypeStruct((DEV * BLOCK, LANES), jnp.float32),
        in_specs=[pl.BlockSpec(memory_space=pltpu.HBM)] * 3,
        out_specs=VMEM,
        scratch_shapes=[
            pltpu.VMEM((D, TOK), jnp.float32),
            pltpu.VMEM((TOK // LANES, LANES), jnp.int32),
            pltpu.VMEM((TOK // LANES, LANES), jnp.int32),
            pltpu.VMEM((TOK, LANES), jnp.float32),
            pltpu.VMEM((DEV * (BLOCK + SEND - MAIN), LANES), jnp.float32),
            pltpu.VMEM((TOK // LANES, LANES), jnp.int32),
            pltpu.SMEM((TOK // LANES, LANES), jnp.int32),
            pltpu.SemaphoreType.DMA((4,)),
        ],
        compiler_params=pltpu.CompilerParams(vmem_limit_bytes=GRANT),
        name="dispatch",
    )(*(pltpu.with_memory_space_constraint(x, pltpu.HBM) for x in arrays))


def place_kernel(got_ref, old_ref, prior_ref, res_hbm, stat_ref, energy_ref, res_ref, cells, tails, lab_v, lab_s, sem, out_sem):
    f32, i32 = jnp.float32, jnp.int32
    lab_v[...] = got_ref[pl.ds(MAIN, DEV, stride=BLOCK), :].astype(i32)
    copy = pltpu.make_async_copy(lab_v, lab_s, sem)
    copy.start()
    cells[...] = jnp.full(cells.shape, jnp.inf, f32)
    near = lax.broadcasted_iota(i32, (8, LANES), 1)

    def unpack(d, carry):
        first, second, third = (
            pltpu.roll(got_ref[pl.ds(d * BLOCK + 8 * k, 8), :], 32 * k + 32, 1) for k in range(MAIN // 8)
        )
        tail = jnp.where(near < 32, first, jnp.where(near < 64, second, third))
        tails[pl.ds(pl.multiple_of(d * (SEND - MAIN), 8), 8), :] = tail
        return carry

    lax.fori_loop(0, DEV, unpack, 0, unroll=8)
    copy.wait()

    def move(d, carry):
        for r in range(MAIN):
            cells[pl.ds(lab_s[d, r], 1), :] = got_ref[pl.ds(d * BLOCK + r, 1), :]
        for r in range(MAIN, SEND):
            cells[pl.ds(lab_s[d, r], 1), :] = tails[pl.ds(d * (SEND - MAIN) + r - MAIN, 1), :]
        return carry

    lax.fori_loop(0, DEV, move, 0, unroll=True)
    lane = lax.broadcasted_iota(i32, (D, LANES), 1)
    to_lane = jnp.bitwise_and(lane, 15) * 8 + lax.shift_right_logical(lane, 4)
    total = jnp.zeros((8, LANES), f32)
    outs = []
    gathered = []
    part = 4

    def send(h, planes):
        outs.append(
            pltpu.make_async_copy(res_ref.at[h, planes], res_hbm.at[h, planes], out_sem.at[len(outs)])
        )
        outs[-1].start()

    for h in range(LISTS // LANES):
        span = slice(h * LANES, (h + 1) * LANES)
        sums = jnp.zeros((D, LANES), f32)
        counts = jnp.zeros((1, LANES), f32)
        seen = []
        for j in range(CAP):
            start = j * LISTS + h * LANES
            block = cells[start : start + LANES, :].T[:D]
            full = block[:1] < jnp.inf
            block = jnp.where(full, block, 0.0)
            here = jnp.where(full, 1.0, 0.0)
            sums = sums + block
            counts = counts + here
            seen.append(here)
            res_ref[h, j] = block
            if j % part == part - 1:
                send(h, slice(j + 1 - part, j + 1))
        prior8 = jnp.broadcast_to(prior_ref[:, span].astype(f32), (8, LANES))
        prior = jnp.take_along_axis(prior8, to_lane[:8], axis=1)[:1]
        old = jnp.take_along_axis(old_ref[:, span], to_lane, axis=1)
        weight = prior + counts
        cent = (prior * old + sums) / weight
        res_ref[h, CAP] = cent
        res_ref[h, CAP + 1, :CAP] = jnp.concatenate(seen, axis=0)
        res_ref[h, CAP + 1, CAP:] = jnp.zeros((D - CAP, LANES), f32)
        stat_ref[:, span] = jnp.concatenate([prior, weight, jnp.zeros((6, LANES), f32)], axis=0)
        send(h, slice(CAP, CAP + 2))
        gathered.append((cent, seen))
    for h, (cent, seen) in enumerate(gathered):
        span = slice(h * LANES, (h + 1) * LANES)
        for j in range(CAP):
            res = res_ref[h, j] - cent * seen[j]
            square = res * res
            for t in range(D // 8):
                total = total + square[8 * t : 8 * t + 8]
    energy_ref[...] = jnp.broadcast_to(jnp.sum(total, axis=0, keepdims=True), (DEV, LANES))
    for out in outs:
        out.wait()


def place(got, old_centroids, prior_counts):
    f32 = jnp.float32
    return pl.pallas_call(
        place_kernel,
        out_shape=(
            pltpu.HBM((LISTS // LANES, CAP + 2, D, LANES), f32),
            jax.ShapeDtypeStruct((8, LISTS), f32),
            jax.ShapeDtypeStruct((DEV, LANES), f32),
        ),
        in_specs=[VMEM] * 3,
        out_specs=(HBM, VMEM, VMEM),
        scratch_shapes=[
            pltpu.VMEM((LISTS // LANES, CAP + 2, D, LANES), f32),
            pltpu.VMEM((CELLS + 8, LANES), f32),
            pltpu.VMEM((DEV * (SEND - MAIN), LANES), f32),
            pltpu.VMEM((DEV, LANES), jnp.int32),
            pltpu.SMEM((DEV, LANES), jnp.int32),
            pltpu.SemaphoreType.DMA,
            pltpu.SemaphoreType.DMA((10,)),
        ],
        compiler_params=pltpu.CompilerParams(vmem_limit_bytes=GRANT),
        name="place",
    )(got, old_centroids, prior_counts.reshape(1, LISTS))


def weave(parts, lane):
    parts = list(parts)
    for bit in (8, 4, 2, 1):
        low = jnp.bitwise_and(lane, bit) == 0
        for j in range(CAP):
            if j & bit == 0:
                one, two = parts[j], parts[j | bit]
                parts[j] = jnp.where(low, one, pltpu.roll(two, bit, 1))
                parts[j | bit] = jnp.where(low, pltpu.roll(one, LANES - bit, 1), two)
    return parts


def times(left, i, right):
    total = left[i, 0:1, :] * right[0]
    for k in range(1, CAP):
        total = total + left[i, k : k + 1, :] * right[k]
    return total


def gram_kernel(res_hbm, woven_ref, out_ref, gram_ref, next_ref, res_ref, sem):
    f32, i32 = jnp.float32, jnp.int32
    get = pltpu.make_async_copy(res_hbm, res_ref, sem)
    get.start()
    get.wait()
    lane = lax.broadcasted_iota(i32, (D, LANES), 1)
    to_list = jnp.bitwise_and(lane, 7) * 16 + lax.shift_right_logical(lane, 3)
    for h in range(LISTS // LANES):
        span = slice(h * LANES, (h + 1) * LANES)
        cent = res_ref[h, CAP]
        out_ref[:, span] = jnp.take_along_axis(cent, to_list, axis=1)
        for j in range(CAP):
            res_ref[h, j] = res_ref[h, j] - cent * res_ref[h, CAP + 1, j : j + 1]

    def row(i, carry):
        for h in range(LISTS // LANES):
            span = slice(h * LANES, (h + 1) * LANES)
            left = res_ref[h, i]
            for step in range(CAP // 2 + 1):
                j = jnp.bitwise_and(i + step, CAP - 1)
                value = jnp.sum(left * res_ref[h, j], axis=0, keepdims=True)
                gram_ref[h, i, pl.ds(j, 1), :] = value
                gram_ref[h, j, pl.ds(i, 1), :] = value
        return carry

    lax.fori_loop(0, CAP, row, 0)

    def spread(t, carry):
        tile = pl.ds(pl.multiple_of(t * 8, 8), 8)
        for h in range(LISTS // LANES):
            span = slice(h * LANES, (h + 1) * LANES)
            parts = weave([res_ref[h, j, tile, :] for j in range(CAP)], lane[:8])
            for j in range(CAP):
                at = (h * CAP + j) * LANES
                woven_ref[tile, at : at + LANES] = parts[j]
        return carry

    lax.fori_loop(0, D // 8, spread, 0)
    group = 4
    for h in range(LISTS // LANES):
        trace = gram_ref[h, 0, 0:1, :]
        for i in range(1, CAP):
            trace = trace + gram_ref[h, i, i : i + 1, :]
        trace = jnp.where(trace > 0.0, trace, 1.0)
        woven_ref[D + POWERS * CAP :, h * LANES : (h + 1) * LANES] = jnp.broadcast_to(trace, (8, LANES))
        unit = 1.0 / trace
        base = []
        for i in range(CAP):
            row = gram_ref[h, i] * unit
            base.append(row)
            next_ref[0, i] = row
            at = (h * CAP + i) * LANES
            woven_ref[D : D + CAP, at : at + LANES] = row

        def raise_rows(block, carry, h=h, base=base):
            spots = [block * group + g for g in range(group)]
            for power in range(1, POWERS):
                for i in spots:
                    row = times(next_ref.at[power - 1], i, base)
                    if power < POWERS - 1:
                        next_ref[power, i] = row
                    at = pl.multiple_of((h * CAP + i) * LANES, LANES)
                    woven_ref[D + power * CAP : D + (power + 1) * CAP, pl.ds(at, LANES)] = row
            return carry

        lax.fori_loop(0, CAP // group, raise_rows, 0)


def gram(res):
    f32 = jnp.float32
    return pl.pallas_call(
        gram_kernel,
        out_shape=(
            jax.ShapeDtypeStruct((D + POWERS * CAP + 8, CELLS), f32),
            jax.ShapeDtypeStruct((D, LISTS), f32),
        ),
        in_specs=[HBM],
        out_specs=(VMEM,) * 2,
        scratch_shapes=[
            pltpu.VMEM((LISTS // LANES, CAP, CAP, LANES), f32),
            pltpu.VMEM((POWERS - 1, CAP, CAP, LANES), f32),
            pltpu.VMEM((LISTS // LANES, CAP + 2, D, LANES), f32),
            pltpu.SemaphoreType.DMA,
        ],
        cost_estimate=pl.CostEstimate(flops=2 * CAP * CAP * D * LISTS, bytes_accessed=8 * CAP * D * LISTS, transcendentals=0),
        compiler_params=pltpu.CompilerParams(vmem_limit_bytes=GRANT),
        name="gram",
    )(pltpu.with_memory_space_constraint(res, pltpu.HBM))


def whiten_kernel(woven_ref, stat_ref, energy_ref, out_hbm, t_ref, z_ref, s_ref, q_ref, w_ref, out_ref, sem):
    f32, bf16, i32 = jnp.float32, jnp.bfloat16, jnp.int32
    group = 4
    row_of = lax.broadcasted_iota(i32, (CAP, LANES), 0)
    energy = jnp.sum(energy_ref[...], axis=(0, 1), keepdims=True)
    shrinkage = shrink_weight * energy / TOTAL + epsilon
    for h in range(LISTS // LANES):
        span = slice(h * LANES, (h + 1) * LANES)
        prior, weight = stat_ref[0:1, span], stat_ref[1:2, span]
        trace = woven_ref[D + POWERS * CAP : D + POWERS * CAP + 1, span]
        share = 1.0 / weight
        ridge = shrinkage * prior * share
        trace = trace * share

        def power(k, i):
            at = (h * CAP + i) * LANES
            return woven_ref[D + k * CAP : D + (k + 1) * CAP, at : at + LANES]

        frob = jnp.zeros((CAP, LANES), f32)
        for i in range(CAP):
            row = trace * power(0, i) + jnp.where(row_of == i, ridge, 0.0)
            frob = frob + row * row
        frob = jnp.sqrt(jnp.sum(frob, axis=0, keepdims=True) + TAIL * (ridge * ridge))
        scale = 1.0 / frob
        a, x = trace * scale, ridge * scale
        t0 = x * (2.25 + x * (0.25 * x - 1.5))
        t1 = a * (2.25 + x * (0.75 * x - 3.0))
        t2 = a * a * (0.75 * x - 1.5)
        t3 = a * a * a * 0.25
        z0 = 2.25 + x * (-2.4375 + x * (1.6875 + x * (0.0625 * x - 0.5625)))
        z1 = a * (-2.4375 + x * (3.375 + x * (0.25 * x - 1.6875)))
        z2 = a * a * (1.6875 + x * (0.375 * x - 1.6875))
        z3 = a * a * a * (0.25 * x - 0.5625)
        z4 = a * a * (a * a) * 0.0625
        middle = []
        for i in range(CAP):
            own = row_of == i
            h1, h2, h3, h4 = (power(k, i) for k in range(POWERS))
            row = t1 * h1 + t2 * h2 + t3 * h3 + jnp.where(own, t0, 0.0)
            t_ref[i] = row
            z_ref[i] = z1 * h1 + z2 * h2 + z3 * h3 + z4 * h4 + jnp.where(own, z0, 0.0)
            middle.append(jnp.where(own, 1.5, 0.0) - 0.5 * row)
        root = 1.0 / jnp.sqrt(frob)

        for step in range(1, STEPS):

            def advance(block, carry, step=step, middle=middle, root=root, h=h):
                spots = [block * group + g for g in range(group)]
                if step < STEPS - 1:
                    for i in spots:
                        s_ref[i] = times(t_ref, i, middle)
                if step > 1:
                    for i in spots:
                        moved = times(z_ref, i, middle)
                        if step == STEPS - 1:
                            q_ref[h, i] = moved * root
                        else:
                            z_ref[i] = moved
                if step < STEPS - 1:
                    for i in spots:
                        t_ref[i] = times(s_ref, i, middle)
                return carry

            lax.fori_loop(0, CAP // group, advance, 0)
            if step < STEPS - 1:
                middle = [jnp.where(row_of == i, 1.5, 0.0) - 0.5 * t_ref[i] for i in range(CAP)]

    lane = lax.broadcasted_iota(i32, (CAP, LANES), 1)
    for h in range(LISTS // LANES):
        for j, part in enumerate(weave([q_ref[h, i] for i in range(CAP)], lane)):
            w_ref[h * CAP + j] = part
    wide = 2 * LANES
    block = lax.broadcasted_iota(i32, (LANES, LANES), 0) // CAP == lax.broadcasted_iota(i32, (LANES, LANES), 1) // CAP
    empty = jnp.zeros((LANES, LANES), bf16)

    def diagonal(first, second):
        first, second = (
            jnp.where(block, jnp.concatenate([x] * (LANES // CAP), axis=0), 0.0).astype(bf16) for x in (first, second)
        )
        return jnp.concatenate(
            [jnp.concatenate([first, empty], axis=1), jnp.concatenate([empty, second], axis=1)], axis=0
        )

    copies = []
    for g in range(CELLS // wide):
        span = slice(g * wide, (g + 1) * wide)
        pair = [w_ref[2 * g], w_ref[2 * g + 1]]
        coarse = [x.astype(bf16).astype(f32) for x in pair]
        fine = [x - y for x, y in zip(pair, coarse)]
        coarse, fine = diagonal(*coarse), diagonal(*fine)
        value = woven_ref[:D, span]
        high = value.astype(bf16)
        low = (value - high.astype(f32)).astype(bf16)
        both = jnp.dot(jnp.concatenate([high, low], axis=0), coarse, preferred_element_type=f32)
        out_ref[:, span] = both[:D] + both[D:] + jnp.dot(high, fine, preferred_element_type=f32)
        copies.append(pltpu.make_async_copy(out_ref.at[:, span], out_hbm.at[:, span], sem.at[g]))
        copies[g].start()
    for copy in copies:
        copy.wait()


def whiten(woven, stat, energy):
    f32 = jnp.float32
    return pl.pallas_call(
        whiten_kernel,
        out_shape=jax.ShapeDtypeStruct((D, CELLS), f32),
        in_specs=[VMEM] * 3,
        out_specs=pl.BlockSpec(memory_space=pltpu.HBM),
        scratch_shapes=[pltpu.VMEM((CAP, CAP, LANES), f32)] * 3
        + [
            pltpu.VMEM((LISTS // LANES, CAP, CAP, LANES), f32),
            pltpu.VMEM((CELLS // LANES, CAP, LANES), f32),
            pltpu.VMEM((D, CELLS), f32),
            pltpu.SemaphoreType.DMA((CELLS // (2 * LANES),)),
        ],
        compiler_params=pltpu.CompilerParams(vmem_limit_bytes=GRANT),
        name="whiten",
    )(woven, stat, energy)


def local(vectors, assignment, slot, old_centroids, prior_counts):
    outgoing = dispatch(vectors, assignment, slot).reshape(DEV, 1, BLOCK * LANES)
    incoming = lax.all_to_all(outgoing, AXES, split_axis=0, concat_axis=0, tiled=True)
    res, stat, energy = place(incoming.reshape(DEV * BLOCK, LANES), old_centroids, prior_counts)
    shared = lax.all_to_all(energy.reshape(DEV, 1, LANES), AXES, split_axis=0, concat_axis=0, tiled=True)
    woven, centroids = gram(res)
    rotated = whiten(woven, stat, shared.reshape(DEV, LANES))
    return (centroids, rotated)


def solution(mesh):
    placed = (
        P(None, AXES),
        P(AXES),
        P(AXES),
        P(None, AXES),
        P(AXES),
    )
    return jax.shard_map(
        local,
        mesh=mesh,
        in_specs=placed,
        out_specs=(P(None, AXES), P(None, AXES)),
        check_vma=False,
    )
```

```python
import jax
import jax.numpy as jnp
from jax import lax
from jax.experimental import pallas as pl
from jax.experimental.pallas import tpu as pltpu
from jax.sharding import PartitionSpec as P

D = 96
CAP = 16
LISTS = 256
CELLS = LISTS * CAP
TOK = 2048
DEV = 128
SEND = 32
STEPS = 4
AXES = ("dp", "owner")
LANES = 128
TAIL = D - CAP
MAIN = 24
BLOCK = MAIN + 1
POWERS = 4
TOTAL = D * TOK * DEV

shrink_weight = 0.5
epsilon = 1e-05

VMEM = pl.BlockSpec(memory_space=pltpu.VMEM)
HBM = pl.BlockSpec(memory_space=pltpu.HBM)
GRANT = 16 * 1024 * 1024


def dispatch_kernel(vec_hbm, assign_hbm, slot_hbm, send_ref, vec_ref, assign_ref, slot_ref, rows, stage, pos_v, pos_s, sem):
    f32, bf16, i32 = jnp.float32, jnp.bfloat16, jnp.int32
    wide = 2 * LANES
    get_assign = pltpu.make_async_copy(assign_hbm, assign_ref, sem.at[0])
    get_slot = pltpu.make_async_copy(slot_hbm, slot_ref, sem.at[1])
    get_vectors = pltpu.make_async_copy(vec_hbm, vec_ref, sem.at[2])
    get_assign.start()
    get_slot.start()
    get_vectors.start()
    get_assign.wait()
    get_slot.wait()
    assign = assign_ref[...]
    owner = lax.shift_right_logical(assign, 8)
    here = jnp.bitwise_and(assign, LISTS - 1)
    half = jnp.bitwise_and(here, LANES - 1)
    lane = jnp.bitwise_and(here, LANES) + jnp.bitwise_and(half, 7) * 16 + lax.shift_right_logical(half, 3)
    code = slot_ref[...] * LISTS + lane + 1
    code_high = lax.shift_right_logical(code, 6).astype(f32)
    code_low = jnp.bitwise_and(code, 63).astype(f32)

    def pair(x, c):
        return jnp.concatenate([x[2 * c : 2 * c + 1, :], x[2 * c + 1 : 2 * c + 2, :]], axis=1)

    sub = lax.broadcasted_iota(i32, (LANES, wide), 0)
    slots = lax.broadcasted_iota(i32, (SEND, wide), 0)
    row2 = lax.broadcasted_iota(i32, (wide, wide), 0)
    col2 = lax.broadcasted_iota(i32, (wide, wide), 1)
    before = jnp.concatenate([jnp.where(row2 < col2, 1.0, 0.0), jnp.ones((wide, wide), f32)], axis=1).astype(bf16)
    picks = [sub == pair(owner, c) for c in range(TOK // wide)]
    hots = [jnp.where(x, 1.0, 0.0).astype(bf16) for x in picks]
    counts = jnp.dot(jnp.concatenate(hots, axis=0), before, preferred_element_type=f32)
    carry = jnp.zeros((LANES, wide), f32)
    codes = jnp.zeros((LANES, 2 * SEND), f32)
    for c in range(TOK // wide):
        mine = pair(owner, c)
        picked, hot = picks[c], hots[c]
        counted = counts[c * LANES : (c + 1) * LANES]
        rank = jnp.sum(jnp.where(picked, counted[:, :wide] + carry, 0.0), axis=0, keepdims=True).astype(i32)
        carry = carry + counted[:, wide:]
        pos = jnp.where(rank < MAIN, mine * BLOCK + rank, DEV * BLOCK - MAIN + mine * (SEND - MAIN) + rank)
        pos_v[2 * c : 2 * c + 1, :] = pos[:, :LANES]
        pos_v[2 * c + 1 : 2 * c + 2, :] = pos[:, LANES:]
        at = slots == rank
        marks = jnp.concatenate(
            [jnp.where(at, pair(code_high, c), 0.0), jnp.where(at, pair(code_low, c), 0.0)], axis=0
        ).astype(bf16)
        codes = codes + lax.dot_general(hot, marks, (((1,), (1,)), ((), ())), preferred_element_type=f32)
    copy = pltpu.make_async_copy(pos_v, pos_s, sem.at[3])
    copy.start()
    labels = codes[:, :SEND] * 64.0 + codes[:, SEND:] - 1.0
    labels = jnp.where(labels < 0.0, float(CELLS), labels)
    labels = jnp.concatenate([labels, jnp.zeros((DEV, LANES - SEND), f32)], axis=1)
    send_ref[pl.ds(MAIN, DEV, stride=BLOCK), :] = labels
    get_vectors.wait()
    for c in range(TOK // LANES):
        block = vec_ref[:, c * LANES : (c + 1) * LANES]
        block = jnp.concatenate([block, block[: LANES - D]], axis=0)
        rows[c * LANES : (c + 1) * LANES, :] = block.T
    copy.wait()

    def move(t, carry):
        stage[pl.ds(pos_s[t // LANES, t % LANES], 1), :] = rows[pl.ds(t, 1), :]
        return carry

    lax.fori_loop(0, TOK, move, 0, unroll=True)
    outer = lax.broadcasted_iota(i32, (8, LANES), 1) >= D

    def pack(d, carry):
        tail = stage[pl.ds(pl.multiple_of(DEV * BLOCK + 8 * d, 8), 8), :]
        for k in range(MAIN // 8):
            spot = pl.ds(d * BLOCK + 8 * k, 8)
            send_ref[spot, :] = jnp.where(outer, pltpu.roll(tail, D - 32 * k, 1) if k else tail, stage[spot, :])
        return carry

    lax.fori_loop(0, DEV, pack, 0, unroll=8)


def dispatch(vectors, assignment, slot):
    arrays = (vectors, assignment.reshape(TOK // LANES, LANES), slot.reshape(TOK // LANES, LANES))
    return pl.pallas_call(
        dispatch_kernel,
        out_shape=jax.ShapeDtypeStruct((DEV * BLOCK, LANES), jnp.float32),
        in_specs=[pl.BlockSpec(memory_space=pltpu.HBM)] * 3,
        out_specs=VMEM,
        scratch_shapes=[
            pltpu.VMEM((D, TOK), jnp.float32),
            pltpu.VMEM((TOK // LANES, LANES), jnp.int32),
            pltpu.VMEM((TOK // LANES, LANES), jnp.int32),
            pltpu.VMEM((TOK, LANES), jnp.float32),
            pltpu.VMEM((DEV * (BLOCK + SEND - MAIN), LANES), jnp.float32),
            pltpu.VMEM((TOK // LANES, LANES), jnp.int32),
            pltpu.SMEM((TOK // LANES, LANES), jnp.int32),
            pltpu.SemaphoreType.DMA((4,)),
        ],
        compiler_params=pltpu.CompilerParams(vmem_limit_bytes=GRANT),
        name="dispatch",
    )(*(pltpu.with_memory_space_constraint(x, pltpu.HBM) for x in arrays))


def place_kernel(got_ref, old_ref, prior_ref, res_hbm, stat_ref, energy_hbm, energy_ref, res_ref, cells, tails, lab_v, lab_s, sem, out_sem):
    f32, i32 = jnp.float32, jnp.int32
    lab_v[...] = got_ref[pl.ds(MAIN, DEV, stride=BLOCK), :].astype(i32)
    copy = pltpu.make_async_copy(lab_v, lab_s, sem)
    copy.start()
    cells[...] = jnp.full(cells.shape, jnp.inf, f32)
    near = lax.broadcasted_iota(i32, (8, LANES), 1)

    def unpack(d, carry):
        first, second, third = (
            pltpu.roll(got_ref[pl.ds(d * BLOCK + 8 * k, 8), :], 32 * k + 32, 1) for k in range(MAIN // 8)
        )
        tail = jnp.where(near < 32, first, jnp.where(near < 64, second, third))
        tails[pl.ds(pl.multiple_of(d * (SEND - MAIN), 8), 8), :] = tail
        return carry

    lax.fori_loop(0, DEV, unpack, 0, unroll=8)
    copy.wait()

    def move(d, carry):
        for r in range(MAIN):
            cells[pl.ds(lab_s[d, r], 1), :] = got_ref[pl.ds(d * BLOCK + r, 1), :]
        for r in range(MAIN, SEND):
            cells[pl.ds(lab_s[d, r], 1), :] = tails[pl.ds(d * (SEND - MAIN) + r - MAIN, 1), :]
        return carry

    lax.fori_loop(0, DEV, move, 0, unroll=True)
    lane = lax.broadcasted_iota(i32, (D, LANES), 1)
    to_lane = jnp.bitwise_and(lane, 15) * 8 + lax.shift_right_logical(lane, 4)
    total = jnp.zeros((8, LANES), f32)
    outs = []
    gathered = []
    part = 4

    def send(h, planes):
        outs.append(
            pltpu.make_async_copy(res_ref.at[h, planes], res_hbm.at[h, planes], out_sem.at[len(outs)])
        )
        outs[-1].start()

    for h in range(LISTS // LANES):
        span = slice(h * LANES, (h + 1) * LANES)
        sums = jnp.zeros((D, LANES), f32)
        counts = jnp.zeros((1, LANES), f32)
        seen = []
        for j in range(CAP):
            start = j * LISTS + h * LANES
            block = cells[start : start + LANES, :].T[:D]
            full = block[:1] < jnp.inf
            block = jnp.where(full, block, 0.0)
            here = jnp.where(full, 1.0, 0.0)
            sums = sums + block
            counts = counts + here
            seen.append(here)
            res_ref[h, j] = block
            if j % part == part - 1:
                send(h, slice(j + 1 - part, j + 1))
        prior8 = jnp.broadcast_to(prior_ref[:, span].astype(f32), (8, LANES))
        prior = jnp.take_along_axis(prior8, to_lane[:8], axis=1)[:1]
        old = jnp.take_along_axis(old_ref[:, span], to_lane, axis=1)
        weight = prior + counts
        cent = (prior * old + sums) / weight
        res_ref[h, CAP] = cent
        res_ref[h, CAP + 1, :CAP] = jnp.concatenate(seen, axis=0)
        res_ref[h, CAP + 1, CAP:] = jnp.zeros((D - CAP, LANES), f32)
        stat_ref[:, span] = jnp.concatenate([prior, weight, jnp.zeros((6, LANES), f32)], axis=0)
        send(h, slice(CAP, CAP + 2))
        gathered.append((cent, seen))
    for h, (cent, seen) in enumerate(gathered):
        span = slice(h * LANES, (h + 1) * LANES)
        for j in range(CAP):
            res = res_ref[h, j] - cent * seen[j]
            square = res * res
            for t in range(D // 8):
                total = total + square[8 * t : 8 * t + 8]
    energy_ref[...] = jnp.broadcast_to(jnp.sum(total, axis=0, keepdims=True), (DEV, LANES))
    outs.append(pltpu.make_async_copy(energy_ref, energy_hbm, out_sem.at[len(outs)]))
    outs[-1].start()
    for out in outs:
        out.wait()


def place(got, old_centroids, prior_counts):
    f32 = jnp.float32
    return pl.pallas_call(
        place_kernel,
        out_shape=(
            pltpu.HBM((LISTS // LANES, CAP + 2, D, LANES), f32),
            jax.ShapeDtypeStruct((8, LISTS), f32),
            pltpu.HBM((DEV, LANES), f32),
        ),
        in_specs=[VMEM] * 3,
        out_specs=(HBM, VMEM, HBM),
        scratch_shapes=[
            pltpu.VMEM((DEV, LANES), f32),
            pltpu.VMEM((LISTS // LANES, CAP + 2, D, LANES), f32),
            pltpu.VMEM((CELLS + 8, LANES), f32),
            pltpu.VMEM((DEV * (SEND - MAIN), LANES), f32),
            pltpu.VMEM((DEV, LANES), jnp.int32),
            pltpu.SMEM((DEV, LANES), jnp.int32),
            pltpu.SemaphoreType.DMA,
            pltpu.SemaphoreType.DMA((11,)),
        ],
        compiler_params=pltpu.CompilerParams(vmem_limit_bytes=GRANT),
        name="place",
    )(got, old_centroids, prior_counts.reshape(1, LISTS))


def weave(parts, lane):
    parts = list(parts)
    for bit in (8, 4, 2, 1):
        low = jnp.bitwise_and(lane, bit) == 0
        for j in range(CAP):
            if j & bit == 0:
                one, two = parts[j], parts[j | bit]
                parts[j] = jnp.where(low, one, pltpu.roll(two, bit, 1))
                parts[j | bit] = jnp.where(low, pltpu.roll(one, LANES - bit, 1), two)
    return parts


def times(left, i, right):
    total = left[i, 0:1, :] * right[0]
    for k in range(1, CAP):
        total = total + left[i, k : k + 1, :] * right[k]
    return total


def gram_kernel(res_hbm, woven_ref, out_ref, gram_ref, next_ref, res_ref, sem):
    f32, i32 = jnp.float32, jnp.int32
    get = pltpu.make_async_copy(res_hbm, res_ref, sem)
    get.start()
    get.wait()
    lane = lax.broadcasted_iota(i32, (D, LANES), 1)
    to_list = jnp.bitwise_and(lane, 7) * 16 + lax.shift_right_logical(lane, 3)
    for h in range(LISTS // LANES):
        span = slice(h * LANES, (h + 1) * LANES)
        cent = res_ref[h, CAP]
        out_ref[:, span] = jnp.take_along_axis(cent, to_list, axis=1)
        for j in range(CAP):
            res_ref[h, j] = res_ref[h, j] - cent * res_ref[h, CAP + 1, j : j + 1]

    def row(i, carry):
        for h in range(LISTS // LANES):
            span = slice(h * LANES, (h + 1) * LANES)
            left = res_ref[h, i]
            for step in range(CAP // 2 + 1):
                j = jnp.bitwise_and(i + step, CAP - 1)
                value = jnp.sum(left * res_ref[h, j], axis=0, keepdims=True)
                gram_ref[h, i, pl.ds(j, 1), :] = value
                gram_ref[h, j, pl.ds(i, 1), :] = value
        return carry

    lax.fori_loop(0, CAP, row, 0)

    def spread(t, carry):
        tile = pl.ds(pl.multiple_of(t * 8, 8), 8)
        for h in range(LISTS // LANES):
            span = slice(h * LANES, (h + 1) * LANES)
            parts = weave([res_ref[h, j, tile, :] for j in range(CAP)], lane[:8])
            for j in range(CAP):
                at = (h * CAP + j) * LANES
                woven_ref[tile, at : at + LANES] = parts[j]
        return carry

    lax.fori_loop(0, D // 8, spread, 0)
    group = 4
    for h in range(LISTS // LANES):
        trace = gram_ref[h, 0, 0:1, :]
        for i in range(1, CAP):
            trace = trace + gram_ref[h, i, i : i + 1, :]
        trace = jnp.where(trace > 0.0, trace, 1.0)
        woven_ref[D + POWERS * CAP :, h * LANES : (h + 1) * LANES] = jnp.broadcast_to(trace, (8, LANES))
        unit = 1.0 / trace
        base = []
        for i in range(CAP):
            row = gram_ref[h, i] * unit
            base.append(row)
            next_ref[0, i] = row
            at = (h * CAP + i) * LANES
            woven_ref[D : D + CAP, at : at + LANES] = row

        def raise_rows(block, carry, h=h, base=base):
            spots = [block * group + g for g in range(group)]
            for power in range(1, POWERS):
                for i in spots:
                    row = times(next_ref.at[power - 1], i, base)
                    if power < POWERS - 1:
                        next_ref[power, i] = row
                    at = pl.multiple_of((h * CAP + i) * LANES, LANES)
                    woven_ref[D + power * CAP : D + (power + 1) * CAP, pl.ds(at, LANES)] = row
            return carry

        lax.fori_loop(0, CAP // group, raise_rows, 0)


def gram(res):
    f32 = jnp.float32
    return pl.pallas_call(
        gram_kernel,
        out_shape=(
            jax.ShapeDtypeStruct((D + POWERS * CAP + 8, CELLS), f32),
            jax.ShapeDtypeStruct((D, LISTS), f32),
        ),
        in_specs=[HBM],
        out_specs=(VMEM,) * 2,
        scratch_shapes=[
            pltpu.VMEM((LISTS // LANES, CAP, CAP, LANES), f32),
            pltpu.VMEM((POWERS - 1, CAP, CAP, LANES), f32),
            pltpu.VMEM((LISTS // LANES, CAP + 2, D, LANES), f32),
            pltpu.SemaphoreType.DMA,
        ],
        cost_estimate=pl.CostEstimate(flops=2 * CAP * CAP * D * LISTS, bytes_accessed=8 * CAP * D * LISTS, transcendentals=0),
        compiler_params=pltpu.CompilerParams(vmem_limit_bytes=GRANT),
        name="gram",
    )(pltpu.with_memory_space_constraint(res, pltpu.HBM))


def whiten_kernel(woven_ref, stat_ref, energy_ref, out_hbm, t_ref, z_ref, s_ref, q_ref, w_ref, out_ref, sem):
    f32, bf16, i32 = jnp.float32, jnp.bfloat16, jnp.int32
    group = 4
    row_of = lax.broadcasted_iota(i32, (CAP, LANES), 0)
    energy = jnp.sum(energy_ref[...], axis=(0, 1), keepdims=True)
    shrinkage = shrink_weight * energy / TOTAL + epsilon
    for h in range(LISTS // LANES):
        span = slice(h * LANES, (h + 1) * LANES)
        prior, weight = stat_ref[0:1, span], stat_ref[1:2, span]
        trace = woven_ref[D + POWERS * CAP : D + POWERS * CAP + 1, span]
        share = 1.0 / weight
        ridge = shrinkage * prior * share
        trace = trace * share

        def power(k, i):
            at = (h * CAP + i) * LANES
            return woven_ref[D + k * CAP : D + (k + 1) * CAP, at : at + LANES]

        frob = jnp.zeros((CAP, LANES), f32)
        for i in range(CAP):
            row = trace * power(0, i) + jnp.where(row_of == i, ridge, 0.0)
            frob = frob + row * row
        frob = jnp.sqrt(jnp.sum(frob, axis=0, keepdims=True) + TAIL * (ridge * ridge))
        scale = 1.0 / frob
        a, x = trace * scale, ridge * scale
        t0 = x * (2.25 + x * (0.25 * x - 1.5))
        t1 = a * (2.25 + x * (0.75 * x - 3.0))
        t2 = a * a * (0.75 * x - 1.5)
        t3 = a * a * a * 0.25
        z0 = 2.25 + x * (-2.4375 + x * (1.6875 + x * (0.0625 * x - 0.5625)))
        z1 = a * (-2.4375 + x * (3.375 + x * (0.25 * x - 1.6875)))
        z2 = a * a * (1.6875 + x * (0.375 * x - 1.6875))
        z3 = a * a * a * (0.25 * x - 0.5625)
        z4 = a * a * (a * a) * 0.0625
        middle = []
        for i in range(CAP):
            own = row_of == i
            h1, h2, h3, h4 = (power(k, i) for k in range(POWERS))
            row = t1 * h1 + t2 * h2 + t3 * h3 + jnp.where(own, t0, 0.0)
            t_ref[i] = row
            z_ref[i] = z1 * h1 + z2 * h2 + z3 * h3 + z4 * h4 + jnp.where(own, z0, 0.0)
            middle.append(jnp.where(own, 1.5, 0.0) - 0.5 * row)
        root = 1.0 / jnp.sqrt(frob)

        for step in range(1, STEPS):

            def advance(block, carry, step=step, middle=middle, root=root, h=h):
                spots = [block * group + g for g in range(group)]
                if step < STEPS - 1:
                    for i in spots:
                        s_ref[i] = times(t_ref, i, middle)
                if step > 1:
                    for i in spots:
                        moved = times(z_ref, i, middle)
                        if step == STEPS - 1:
                            q_ref[h, i] = moved * root
                        else:
                            z_ref[i] = moved
                if step < STEPS - 1:
                    for i in spots:
                        t_ref[i] = times(s_ref, i, middle)
                return carry

            lax.fori_loop(0, CAP // group, advance, 0)
            if step < STEPS - 1:
                middle = [jnp.where(row_of == i, 1.5, 0.0) - 0.5 * t_ref[i] for i in range(CAP)]

    lane = lax.broadcasted_iota(i32, (CAP, LANES), 1)
    for h in range(LISTS // LANES):
        for j, part in enumerate(weave([q_ref[h, i] for i in range(CAP)], lane)):
            w_ref[h * CAP + j] = part
    wide = 2 * LANES
    block = lax.broadcasted_iota(i32, (LANES, LANES), 0) // CAP == lax.broadcasted_iota(i32, (LANES, LANES), 1) // CAP
    empty = jnp.zeros((LANES, LANES), bf16)

    def diagonal(first, second):
        first, second = (
            jnp.where(block, jnp.concatenate([x] * (LANES // CAP), axis=0), 0.0).astype(bf16) for x in (first, second)
        )
        return jnp.concatenate(
            [jnp.concatenate([first, empty], axis=1), jnp.concatenate([empty, second], axis=1)], axis=0
        )

    copies = []
    for g in range(CELLS // wide):
        span = slice(g * wide, (g + 1) * wide)
        pair = [w_ref[2 * g], w_ref[2 * g + 1]]
        coarse = [x.astype(bf16).astype(f32) for x in pair]
        fine = [x - y for x, y in zip(pair, coarse)]
        coarse, fine = diagonal(*coarse), diagonal(*fine)
        value = woven_ref[:D, span]
        high = value.astype(bf16)
        low = (value - high.astype(f32)).astype(bf16)
        both = jnp.dot(jnp.concatenate([high, low], axis=0), coarse, preferred_element_type=f32)
        out_ref[:, span] = both[:D] + both[D:] + jnp.dot(high, fine, preferred_element_type=f32)
        copies.append(pltpu.make_async_copy(out_ref.at[:, span], out_hbm.at[:, span], sem.at[g]))
        copies[g].start()
    for copy in copies:
        copy.wait()


def whiten(woven, stat, energy):
    f32 = jnp.float32
    return pl.pallas_call(
        whiten_kernel,
        out_shape=jax.ShapeDtypeStruct((D, CELLS), f32),
        in_specs=[VMEM] * 3,
        out_specs=pl.BlockSpec(memory_space=pltpu.HBM),
        scratch_shapes=[pltpu.VMEM((CAP, CAP, LANES), f32)] * 3
        + [
            pltpu.VMEM((LISTS // LANES, CAP, CAP, LANES), f32),
            pltpu.VMEM((CELLS // LANES, CAP, LANES), f32),
            pltpu.VMEM((D, CELLS), f32),
            pltpu.SemaphoreType.DMA((CELLS // (2 * LANES),)),
        ],
        compiler_params=pltpu.CompilerParams(vmem_limit_bytes=GRANT),
        name="whiten",
    )(woven, stat, energy)


def local(vectors, assignment, slot, old_centroids, prior_counts):
    outgoing = dispatch(vectors, assignment, slot).reshape(DEV, 1, BLOCK * LANES)
    incoming = lax.all_to_all(outgoing, AXES, split_axis=0, concat_axis=0, tiled=True)
    res, stat, energy = place(incoming.reshape(DEV * BLOCK, LANES), old_centroids, prior_counts)
    shared = lax.all_to_all(energy.reshape(DEV, 1, LANES), AXES, split_axis=0, concat_axis=0, tiled=True)
    woven, centroids = gram(res)
    rotated = whiten(woven, stat, shared.reshape(DEV, LANES))
    return (centroids, rotated)


def solution(mesh):
    placed = (
        P(None, AXES),
        P(AXES),
        P(AXES),
        P(None, AXES),
        P(AXES),
    )
    return jax.shard_map(
        local,
        mesh=mesh,
        in_specs=placed,
        out_specs=(P(None, AXES), P(None, AXES)),
        check_vma=False,
    )
```

```python
import jax
import jax.numpy as jnp
from jax import lax
from jax.experimental import pallas as pl
from jax.experimental.pallas import tpu as pltpu
from jax.sharding import PartitionSpec as P

D = 96
CAP = 16
LISTS = 256
CELLS = LISTS * CAP
TOK = 2048
DEV = 128
SEND = 32
STEPS = 4
AXES = ("dp", "owner")
EXCHANGE = ("owner", "dp")
OWNERS = 8
LANES = 128
TAIL = D - CAP
MAIN = 24
BLOCK = MAIN + 1
POWERS = 4
TOTAL = D * TOK * DEV

shrink_weight = 0.5
epsilon = 1e-05

VMEM = pl.BlockSpec(memory_space=pltpu.VMEM)
HBM = pl.BlockSpec(memory_space=pltpu.HBM)
GRANT = 16 * 1024 * 1024


def dispatch_kernel(vec_hbm, assign_hbm, slot_hbm, send_ref, vec_ref, assign_ref, slot_ref, rows, stage, pos_v, pos_s, sem):
    f32, bf16, i32 = jnp.float32, jnp.bfloat16, jnp.int32
    wide = 2 * LANES
    get_assign = pltpu.make_async_copy(assign_hbm, assign_ref, sem.at[0])
    get_slot = pltpu.make_async_copy(slot_hbm, slot_ref, sem.at[1])
    get_vectors = pltpu.make_async_copy(vec_hbm, vec_ref, sem.at[2])
    get_assign.start()
    get_slot.start()
    get_vectors.start()
    get_assign.wait()
    get_slot.wait()
    assign = assign_ref[...]
    device = lax.shift_right_logical(assign, 8)
    owner = jnp.bitwise_and(device, OWNERS - 1) * (DEV // OWNERS) + lax.shift_right_logical(device, 3)
    here = jnp.bitwise_and(assign, LISTS - 1)
    half = jnp.bitwise_and(here, LANES - 1)
    lane = jnp.bitwise_and(here, LANES) + jnp.bitwise_and(half, 7) * 16 + lax.shift_right_logical(half, 3)
    code = slot_ref[...] * LISTS + lane + 1
    code_high = lax.shift_right_logical(code, 6).astype(f32)
    code_low = jnp.bitwise_and(code, 63).astype(f32)

    def pair(x, c):
        return jnp.concatenate([x[2 * c : 2 * c + 1, :], x[2 * c + 1 : 2 * c + 2, :]], axis=1)

    sub = lax.broadcasted_iota(i32, (LANES, wide), 0)
    slots = lax.broadcasted_iota(i32, (SEND, wide), 0)
    row2 = lax.broadcasted_iota(i32, (wide, wide), 0)
    col2 = lax.broadcasted_iota(i32, (wide, wide), 1)
    before = jnp.concatenate([jnp.where(row2 < col2, 1.0, 0.0), jnp.ones((wide, wide), f32)], axis=1).astype(bf16)
    picks = [sub == pair(owner, c) for c in range(TOK // wide)]
    hots = [jnp.where(x, 1.0, 0.0).astype(bf16) for x in picks]
    counts = jnp.dot(jnp.concatenate(hots, axis=0), before, preferred_element_type=f32)
    carry = jnp.zeros((LANES, wide), f32)
    codes = jnp.zeros((LANES, 2 * SEND), f32)
    for c in range(TOK // wide):
        mine = pair(owner, c)
        picked, hot = picks[c], hots[c]
        counted = counts[c * LANES : (c + 1) * LANES]
        rank = jnp.sum(jnp.where(picked, counted[:, :wide] + carry, 0.0), axis=0, keepdims=True).astype(i32)
        carry = carry + counted[:, wide:]
        pos = jnp.where(rank < MAIN, mine * BLOCK + rank, DEV * BLOCK - MAIN + mine * (SEND - MAIN) + rank)
        pos_v[2 * c : 2 * c + 1, :] = pos[:, :LANES]
        pos_v[2 * c + 1 : 2 * c + 2, :] = pos[:, LANES:]
        at = slots == rank
        marks = jnp.concatenate(
            [jnp.where(at, pair(code_high, c), 0.0), jnp.where(at, pair(code_low, c), 0.0)], axis=0
        ).astype(bf16)
        codes = codes + lax.dot_general(hot, marks, (((1,), (1,)), ((), ())), preferred_element_type=f32)
    copy = pltpu.make_async_copy(pos_v, pos_s, sem.at[3])
    copy.start()
    labels = codes[:, :SEND] * 64.0 + codes[:, SEND:] - 1.0
    labels = jnp.where(labels < 0.0, float(CELLS), labels)
    labels = jnp.concatenate([labels, jnp.zeros((DEV, LANES - SEND), f32)], axis=1)
    send_ref[pl.ds(MAIN, DEV, stride=BLOCK), :] = labels
    get_vectors.wait()
    for c in range(TOK // LANES):
        block = vec_ref[:, c * LANES : (c + 1) * LANES]
        block = jnp.concatenate([block, block[: LANES - D]], axis=0)
        rows[c * LANES : (c + 1) * LANES, :] = block.T
    copy.wait()

    def move(t, carry):
        stage[pl.ds(pos_s[t // LANES, t % LANES], 1), :] = rows[pl.ds(t, 1), :]
        return carry

    lax.fori_loop(0, TOK, move, 0, unroll=True)
    outer = lax.broadcasted_iota(i32, (8, LANES), 1) >= D

    def pack(d, carry):
        tail = stage[pl.ds(pl.multiple_of(DEV * BLOCK + 8 * d, 8), 8), :]
        for k in range(MAIN // 8):
            spot = pl.ds(d * BLOCK + 8 * k, 8)
            send_ref[spot, :] = jnp.where(outer, pltpu.roll(tail, D - 32 * k, 1) if k else tail, stage[spot, :])
        return carry

    lax.fori_loop(0, DEV, pack, 0, unroll=8)


def dispatch(vectors, assignment, slot):
    arrays = (vectors, assignment.reshape(TOK // LANES, LANES), slot.reshape(TOK // LANES, LANES))
    return pl.pallas_call(
        dispatch_kernel,
        out_shape=jax.ShapeDtypeStruct((DEV * BLOCK, LANES), jnp.float32),
        in_specs=[pl.BlockSpec(memory_space=pltpu.HBM)] * 3,
        out_specs=VMEM,
        scratch_shapes=[
            pltpu.VMEM((D, TOK), jnp.float32),
            pltpu.VMEM((TOK // LANES, LANES), jnp.int32),
            pltpu.VMEM((TOK // LANES, LANES), jnp.int32),
            pltpu.VMEM((TOK, LANES), jnp.float32),
            pltpu.VMEM((DEV * (BLOCK + SEND - MAIN), LANES), jnp.float32),
            pltpu.VMEM((TOK // LANES, LANES), jnp.int32),
            pltpu.SMEM((TOK // LANES, LANES), jnp.int32),
            pltpu.SemaphoreType.DMA((4,)),
        ],
        compiler_params=pltpu.CompilerParams(vmem_limit_bytes=GRANT),
        name="dispatch",
    )(*(pltpu.with_memory_space_constraint(x, pltpu.HBM) for x in arrays))


def place_kernel(got_ref, old_ref, prior_ref, res_hbm, stat_ref, energy_hbm, energy_ref, res_ref, cells, tails, lab_v, lab_s, sem, out_sem):
    f32, i32 = jnp.float32, jnp.int32
    lab_v[...] = got_ref[pl.ds(MAIN, DEV, stride=BLOCK), :].astype(i32)
    copy = pltpu.make_async_copy(lab_v, lab_s, sem)
    copy.start()
    cells[...] = jnp.full(cells.shape, jnp.inf, f32)
    near = lax.broadcasted_iota(i32, (8, LANES), 1)

    def unpack(d, carry):
        first, second, third = (
            pltpu.roll(got_ref[pl.ds(d * BLOCK + 8 * k, 8), :], 32 * k + 32, 1) for k in range(MAIN // 8)
        )
        tail = jnp.where(near < 32, first, jnp.where(near < 64, second, third))
        tails[pl.ds(pl.multiple_of(d * (SEND - MAIN), 8), 8), :] = tail
        return carry

    lax.fori_loop(0, DEV, unpack, 0, unroll=8)
    copy.wait()

    def move(d, carry):
        for r in range(MAIN):
            cells[pl.ds(lab_s[d, r], 1), :] = got_ref[pl.ds(d * BLOCK + r, 1), :]
        for r in range(MAIN, SEND):
            cells[pl.ds(lab_s[d, r], 1), :] = tails[pl.ds(d * (SEND - MAIN) + r - MAIN, 1), :]
        return carry

    lax.fori_loop(0, DEV, move, 0, unroll=True)
    lane = lax.broadcasted_iota(i32, (D, LANES), 1)
    to_lane = jnp.bitwise_and(lane, 15) * 8 + lax.shift_right_logical(lane, 4)
    total = jnp.zeros((8, LANES), f32)
    outs = []
    gathered = []
    part = 4

    def send(h, planes):
        outs.append(
            pltpu.make_async_copy(res_ref.at[h, planes], res_hbm.at[h, planes], out_sem.at[len(outs)])
        )
        outs[-1].start()

    for h in range(LISTS // LANES):
        span = slice(h * LANES, (h + 1) * LANES)
        sums = jnp.zeros((D, LANES), f32)
        counts = jnp.zeros((1, LANES), f32)
        seen = []
        for j in range(CAP):
            start = j * LISTS + h * LANES
            block = cells[start : start + LANES, :].T[:D]
            full = block[:1] < jnp.inf
            block = jnp.where(full, block, 0.0)
            here = jnp.where(full, 1.0, 0.0)
            sums = sums + block
            counts = counts + here
            seen.append(here)
            res_ref[h, j] = block
            if j % part == part - 1:
                send(h, slice(j + 1 - part, j + 1))
        prior8 = jnp.broadcast_to(prior_ref[:, span].astype(f32), (8, LANES))
        prior = jnp.take_along_axis(prior8, to_lane[:8], axis=1)[:1]
        old = jnp.take_along_axis(old_ref[:, span], to_lane, axis=1)
        weight = prior + counts
        cent = (prior * old + sums) / weight
        res_ref[h, CAP] = cent
        res_ref[h, CAP + 1, :CAP] = jnp.concatenate(seen, axis=0)
        res_ref[h, CAP + 1, CAP:] = jnp.zeros((D - CAP, LANES), f32)
        stat_ref[:, span] = jnp.concatenate([prior, weight, jnp.zeros((6, LANES), f32)], axis=0)
        send(h, slice(CAP, CAP + 2))
        gathered.append((cent, seen))
    for h, (cent, seen) in enumerate(gathered):
        span = slice(h * LANES, (h + 1) * LANES)
        for j in range(CAP):
            res = res_ref[h, j] - cent * seen[j]
            square = res * res
            for t in range(D // 8):
                total = total + square[8 * t : 8 * t + 8]
    energy_ref[...] = jnp.broadcast_to(jnp.sum(total, axis=0, keepdims=True), (DEV, LANES))
    outs.append(pltpu.make_async_copy(energy_ref, energy_hbm, out_sem.at[len(outs)]))
    outs[-1].start()
    for out in outs:
        out.wait()


def place(got, old_centroids, prior_counts):
    f32 = jnp.float32
    return pl.pallas_call(
        place_kernel,
        out_shape=(
            pltpu.HBM((LISTS // LANES, CAP + 2, D, LANES), f32),
            jax.ShapeDtypeStruct((8, LISTS), f32),
            pltpu.HBM((DEV, LANES), f32),
        ),
        in_specs=[VMEM] * 3,
        out_specs=(HBM, VMEM, HBM),
        scratch_shapes=[
            pltpu.VMEM((DEV, LANES), f32),
            pltpu.VMEM((LISTS // LANES, CAP + 2, D, LANES), f32),
            pltpu.VMEM((CELLS + 8, LANES), f32),
            pltpu.VMEM((DEV * (SEND - MAIN), LANES), f32),
            pltpu.VMEM((DEV, LANES), jnp.int32),
            pltpu.SMEM((DEV, LANES), jnp.int32),
            pltpu.SemaphoreType.DMA,
            pltpu.SemaphoreType.DMA((11,)),
        ],
        compiler_params=pltpu.CompilerParams(vmem_limit_bytes=GRANT),
        name="place",
    )(got, old_centroids, prior_counts.reshape(1, LISTS))


def weave(parts, lane):
    parts = list(parts)
    for bit in (8, 4, 2, 1):
        low = jnp.bitwise_and(lane, bit) == 0
        for j in range(CAP):
            if j & bit == 0:
                one, two = parts[j], parts[j | bit]
                parts[j] = jnp.where(low, one, pltpu.roll(two, bit, 1))
                parts[j | bit] = jnp.where(low, pltpu.roll(one, LANES - bit, 1), two)
    return parts


def times(left, i, right):
    total = left[i, 0:1, :] * right[0]
    for k in range(1, CAP):
        total = total + left[i, k : k + 1, :] * right[k]
    return total


def gram_kernel(res_hbm, woven_ref, out_ref, gram_ref, next_ref, res_ref, sem):
    f32, i32 = jnp.float32, jnp.int32
    get = pltpu.make_async_copy(res_hbm, res_ref, sem)
    get.start()
    get.wait()
    lane = lax.broadcasted_iota(i32, (D, LANES), 1)
    to_list = jnp.bitwise_and(lane, 7) * 16 + lax.shift_right_logical(lane, 3)
    for h in range(LISTS // LANES):
        span = slice(h * LANES, (h + 1) * LANES)
        cent = res_ref[h, CAP]
        out_ref[:, span] = jnp.take_along_axis(cent, to_list, axis=1)
        for j in range(CAP):
            res_ref[h, j] = res_ref[h, j] - cent * res_ref[h, CAP + 1, j : j + 1]

    def row(i, carry):
        for h in range(LISTS // LANES):
            span = slice(h * LANES, (h + 1) * LANES)
            left = res_ref[h, i]
            for step in range(CAP // 2 + 1):
                j = jnp.bitwise_and(i + step, CAP - 1)
                value = jnp.sum(left * res_ref[h, j], axis=0, keepdims=True)
                gram_ref[h, i, pl.ds(j, 1), :] = value
                gram_ref[h, j, pl.ds(i, 1), :] = value
        return carry

    lax.fori_loop(0, CAP, row, 0)

    def spread(t, carry):
        tile = pl.ds(pl.multiple_of(t * 8, 8), 8)
        for h in range(LISTS // LANES):
            span = slice(h * LANES, (h + 1) * LANES)
            parts = weave([res_ref[h, j, tile, :] for j in range(CAP)], lane[:8])
            for j in range(CAP):
                at = (h * CAP + j) * LANES
                woven_ref[tile, at : at + LANES] = parts[j]
        return carry

    lax.fori_loop(0, D // 8, spread, 0)
    group = 4
    for h in range(LISTS // LANES):
        trace = gram_ref[h, 0, 0:1, :]
        for i in range(1, CAP):
            trace = trace + gram_ref[h, i, i : i + 1, :]
        trace = jnp.where(trace > 0.0, trace, 1.0)
        woven_ref[D + POWERS * CAP :, h * LANES : (h + 1) * LANES] = jnp.broadcast_to(trace, (8, LANES))
        unit = 1.0 / trace
        base = []
        for i in range(CAP):
            row = gram_ref[h, i] * unit
            base.append(row)
            next_ref[0, i] = row
            at = (h * CAP + i) * LANES
            woven_ref[D : D + CAP, at : at + LANES] = row

        def raise_rows(block, carry, h=h, base=base):
            spots = [block * group + g for g in range(group)]
            for power in range(1, POWERS):
                for i in spots:
                    row = times(next_ref.at[power - 1], i, base)
                    if power < POWERS - 1:
                        next_ref[power, i] = row
                    at = pl.multiple_of((h * CAP + i) * LANES, LANES)
                    woven_ref[D + power * CAP : D + (power + 1) * CAP, pl.ds(at, LANES)] = row
            return carry

        lax.fori_loop(0, CAP // group, raise_rows, 0)


def gram(res):
    f32 = jnp.float32
    return pl.pallas_call(
        gram_kernel,
        out_shape=(
            jax.ShapeDtypeStruct((D + POWERS * CAP + 8, CELLS), f32),
            jax.ShapeDtypeStruct((D, LISTS), f32),
        ),
        in_specs=[HBM],
        out_specs=(VMEM,) * 2,
        scratch_shapes=[
            pltpu.VMEM((LISTS // LANES, CAP, CAP, LANES), f32),
            pltpu.VMEM((POWERS - 1, CAP, CAP, LANES), f32),
            pltpu.VMEM((LISTS // LANES, CAP + 2, D, LANES), f32),
            pltpu.SemaphoreType.DMA,
        ],
        cost_estimate=pl.CostEstimate(flops=2 * CAP * CAP * D * LISTS, bytes_accessed=8 * CAP * D * LISTS, transcendentals=0),
        compiler_params=pltpu.CompilerParams(vmem_limit_bytes=GRANT),
        name="gram",
    )(pltpu.with_memory_space_constraint(res, pltpu.HBM))


def whiten_kernel(woven_ref, stat_ref, energy_ref, out_hbm, t_ref, z_ref, s_ref, q_ref, w_ref, out_ref, sem):
    f32, bf16, i32 = jnp.float32, jnp.bfloat16, jnp.int32
    group = 4
    row_of = lax.broadcasted_iota(i32, (CAP, LANES), 0)
    energy = jnp.sum(energy_ref[...], axis=(0, 1), keepdims=True)
    shrinkage = shrink_weight * energy / TOTAL + epsilon
    for h in range(LISTS // LANES):
        span = slice(h * LANES, (h + 1) * LANES)
        prior, weight = stat_ref[0:1, span], stat_ref[1:2, span]
        trace = woven_ref[D + POWERS * CAP : D + POWERS * CAP + 1, span]
        share = 1.0 / weight
        ridge = shrinkage * prior * share
        trace = trace * share

        def power(k, i):
            at = (h * CAP + i) * LANES
            return woven_ref[D + k * CAP : D + (k + 1) * CAP, at : at + LANES]

        frob = jnp.zeros((CAP, LANES), f32)
        for i in range(CAP):
            row = trace * power(0, i) + jnp.where(row_of == i, ridge, 0.0)
            frob = frob + row * row
        frob = jnp.sqrt(jnp.sum(frob, axis=0, keepdims=True) + TAIL * (ridge * ridge))
        scale = 1.0 / frob
        a, x = trace * scale, ridge * scale
        t0 = x * (2.25 + x * (0.25 * x - 1.5))
        t1 = a * (2.25 + x * (0.75 * x - 3.0))
        t2 = a * a * (0.75 * x - 1.5)
        t3 = a * a * a * 0.25
        z0 = 2.25 + x * (-2.4375 + x * (1.6875 + x * (0.0625 * x - 0.5625)))
        z1 = a * (-2.4375 + x * (3.375 + x * (0.25 * x - 1.6875)))
        z2 = a * a * (1.6875 + x * (0.375 * x - 1.6875))
        z3 = a * a * a * (0.25 * x - 0.5625)
        z4 = a * a * (a * a) * 0.0625
        middle = []
        for i in range(CAP):
            own = row_of == i
            h1, h2, h3, h4 = (power(k, i) for k in range(POWERS))
            row = t1 * h1 + t2 * h2 + t3 * h3 + jnp.where(own, t0, 0.0)
            t_ref[i] = row
            z_ref[i] = z1 * h1 + z2 * h2 + z3 * h3 + z4 * h4 + jnp.where(own, z0, 0.0)
            middle.append(jnp.where(own, 1.5, 0.0) - 0.5 * row)
        root = 1.0 / jnp.sqrt(frob)

        for step in range(1, STEPS):

            def advance(block, carry, step=step, middle=middle, root=root, h=h):
                spots = [block * group + g for g in range(group)]
                if step < STEPS - 1:
                    for i in spots:
                        s_ref[i] = times(t_ref, i, middle)
                if step > 1:
                    for i in spots:
                        moved = times(z_ref, i, middle)
                        if step == STEPS - 1:
                            q_ref[h, i] = moved * root
                        else:
                            z_ref[i] = moved
                if step < STEPS - 1:
                    for i in spots:
                        t_ref[i] = times(s_ref, i, middle)
                return carry

            lax.fori_loop(0, CAP // group, advance, 0)
            if step < STEPS - 1:
                middle = [jnp.where(row_of == i, 1.5, 0.0) - 0.5 * t_ref[i] for i in range(CAP)]

    lane = lax.broadcasted_iota(i32, (CAP, LANES), 1)
    for h in range(LISTS // LANES):
        for j, part in enumerate(weave([q_ref[h, i] for i in range(CAP)], lane)):
            w_ref[h * CAP + j] = part
    wide = 2 * LANES
    block = lax.broadcasted_iota(i32, (LANES, LANES), 0) // CAP == lax.broadcasted_iota(i32, (LANES, LANES), 1) // CAP
    empty = jnp.zeros((LANES, LANES), bf16)

    def diagonal(first, second):
        first, second = (
            jnp.where(block, jnp.concatenate([x] * (LANES // CAP), axis=0), 0.0).astype(bf16) for x in (first, second)
        )
        return jnp.concatenate(
            [jnp.concatenate([first, empty], axis=1), jnp.concatenate([empty, second], axis=1)], axis=0
        )

    copies = []
    for g in range(CELLS // wide):
        span = slice(g * wide, (g + 1) * wide)
        pair = [w_ref[2 * g], w_ref[2 * g + 1]]
        coarse = [x.astype(bf16).astype(f32) for x in pair]
        fine = [x - y for x, y in zip(pair, coarse)]
        coarse, fine = diagonal(*coarse), diagonal(*fine)
        value = woven_ref[:D, span]
        high = value.astype(bf16)
        low = (value - high.astype(f32)).astype(bf16)
        both = jnp.dot(jnp.concatenate([high, low], axis=0), coarse, preferred_element_type=f32)
        out_ref[:, span] = both[:D] + both[D:] + jnp.dot(high, fine, preferred_element_type=f32)
        copies.append(pltpu.make_async_copy(out_ref.at[:, span], out_hbm.at[:, span], sem.at[g]))
        copies[g].start()
    for copy in copies:
        copy.wait()


def whiten(woven, stat, energy):
    f32 = jnp.float32
    return pl.pallas_call(
        whiten_kernel,
        out_shape=jax.ShapeDtypeStruct((D, CELLS), f32),
        in_specs=[VMEM] * 3,
        out_specs=pl.BlockSpec(memory_space=pltpu.HBM),
        scratch_shapes=[pltpu.VMEM((CAP, CAP, LANES), f32)] * 3
        + [
            pltpu.VMEM((LISTS // LANES, CAP, CAP, LANES), f32),
            pltpu.VMEM((CELLS // LANES, CAP, LANES), f32),
            pltpu.VMEM((D, CELLS), f32),
            pltpu.SemaphoreType.DMA((CELLS // (2 * LANES),)),
        ],
        compiler_params=pltpu.CompilerParams(vmem_limit_bytes=GRANT),
        name="whiten",
    )(woven, stat, energy)


def local(vectors, assignment, slot, old_centroids, prior_counts):
    outgoing = dispatch(vectors, assignment, slot).reshape(DEV, 1, BLOCK * LANES)
    incoming = lax.all_to_all(outgoing, EXCHANGE, split_axis=0, concat_axis=0, tiled=True)
    res, stat, energy = place(incoming.reshape(DEV * BLOCK, LANES), old_centroids, prior_counts)
    shared = lax.all_to_all(energy.reshape(DEV, 1, LANES), EXCHANGE, split_axis=0, concat_axis=0, tiled=True)
    woven, centroids = gram(res)
    rotated = whiten(woven, stat, shared.reshape(DEV, LANES))
    return (centroids, rotated)


def solution(mesh):
    placed = (
        P(None, AXES),
        P(AXES),
        P(AXES),
        P(None, AXES),
        P(AXES),
    )
    return jax.shard_map(
        local,
        mesh=mesh,
        in_specs=placed,
        out_specs=(P(None, AXES), P(None, AXES)),
        check_vma=False,
    )
```

```python
import jax
import jax.numpy as jnp
from jax import lax
from jax.experimental import pallas as pl
from jax.experimental.pallas import tpu as pltpu
from jax.sharding import PartitionSpec as P

D = 96
CAP = 16
LISTS = 256
CELLS = LISTS * CAP
TOK = 2048
DEV = 128
SEND = 32
STEPS = 4
AXES = ("dp", "owner")
LANES = 128
TAIL = D - CAP
MAIN = 24
BLOCK = MAIN + 1
POWERS = 4
TOTAL = D * TOK * DEV

shrink_weight = 0.5
epsilon = 1e-05

VMEM = pl.BlockSpec(memory_space=pltpu.VMEM)
HBM = pl.BlockSpec(memory_space=pltpu.HBM)
GRANT = 16 * 1024 * 1024


def dispatch_kernel(vec_hbm, assign_hbm, slot_hbm, send_ref, vec_ref, assign_ref, slot_ref, rows, stage, pos_v, pos_s, sem):
    f32, bf16, i32 = jnp.float32, jnp.bfloat16, jnp.int32
    wide = 2 * LANES
    get_assign = pltpu.make_async_copy(assign_hbm, assign_ref, sem.at[0])
    get_slot = pltpu.make_async_copy(slot_hbm, slot_ref, sem.at[1])
    get_vectors = pltpu.make_async_copy(vec_hbm, vec_ref, sem.at[2])
    get_assign.start()
    get_slot.start()
    get_vectors.start()
    get_assign.wait()
    get_slot.wait()
    assign = assign_ref[...]
    owner = lax.shift_right_logical(assign, 8)
    here = jnp.bitwise_and(assign, LISTS - 1)
    half = jnp.bitwise_and(here, LANES - 1)
    lane = jnp.bitwise_and(here, LANES) + jnp.bitwise_and(half, 7) * 16 + lax.shift_right_logical(half, 3)
    code = slot_ref[...] * LISTS + lane + 1
    code_high = lax.shift_right_logical(code, 6).astype(f32)
    code_low = jnp.bitwise_and(code, 63).astype(f32)

    def pair(x, c):
        return jnp.concatenate([x[2 * c : 2 * c + 1, :], x[2 * c + 1 : 2 * c + 2, :]], axis=1)

    sub = lax.broadcasted_iota(i32, (LANES, wide), 0)
    slots = lax.broadcasted_iota(i32, (SEND, wide), 0)
    row2 = lax.broadcasted_iota(i32, (wide, wide), 0)
    col2 = lax.broadcasted_iota(i32, (wide, wide), 1)
    before = jnp.concatenate([jnp.where(row2 < col2, 1.0, 0.0), jnp.ones((wide, wide), f32)], axis=1).astype(bf16)
    picks = [sub == pair(owner, c) for c in range(TOK // wide)]
    hots = [jnp.where(x, 1.0, 0.0).astype(bf16) for x in picks]
    counts = jnp.dot(jnp.concatenate(hots, axis=0), before, preferred_element_type=f32)
    carry = jnp.zeros((LANES, wide), f32)
    codes = jnp.zeros((LANES, 2 * SEND), f32)
    for c in range(TOK // wide):
        mine = pair(owner, c)
        picked, hot = picks[c], hots[c]
        counted = counts[c * LANES : (c + 1) * LANES]
        rank = jnp.sum(jnp.where(picked, counted[:, :wide] + carry, 0.0), axis=0, keepdims=True).astype(i32)
        carry = carry + counted[:, wide:]
        pos = jnp.where(rank < MAIN, mine * BLOCK + rank, DEV * BLOCK - MAIN + mine * (SEND - MAIN) + rank)
        pos_v[2 * c : 2 * c + 1, :] = pos[:, :LANES]
        pos_v[2 * c + 1 : 2 * c + 2, :] = pos[:, LANES:]
        at = slots == rank
        marks = jnp.concatenate(
            [jnp.where(at, pair(code_high, c), 0.0), jnp.where(at, pair(code_low, c), 0.0)], axis=0
        ).astype(bf16)
        codes = codes + lax.dot_general(hot, marks, (((1,), (1,)), ((), ())), preferred_element_type=f32)
    copy = pltpu.make_async_copy(pos_v, pos_s, sem.at[3])
    copy.start()
    labels = codes[:, :SEND] * 64.0 + codes[:, SEND:] - 1.0
    labels = jnp.where(labels < 0.0, float(CELLS), labels)
    labels = jnp.concatenate([labels, jnp.zeros((DEV, LANES - SEND), f32)], axis=1)
    send_ref[pl.ds(MAIN, DEV, stride=BLOCK), :] = labels
    get_vectors.wait()
    for c in range(TOK // LANES):
        block = vec_ref[:, c * LANES : (c + 1) * LANES]
        block = jnp.concatenate([block, block[: LANES - D]], axis=0)
        rows[c * LANES : (c + 1) * LANES, :] = block.T
    copy.wait()

    def move(t, carry):
        stage[pl.ds(pos_s[t // LANES, t % LANES], 1), :] = rows[pl.ds(t, 1), :]
        return carry

    lax.fori_loop(0, TOK, move, 0, unroll=True)
    outer = lax.broadcasted_iota(i32, (8, LANES), 1) >= D

    def pack(d, carry):
        tail = stage[pl.ds(pl.multiple_of(DEV * BLOCK + 8 * d, 8), 8), :]
        for k in range(MAIN // 8):
            spot = pl.ds(d * BLOCK + 8 * k, 8)
            send_ref[spot, :] = jnp.where(outer, pltpu.roll(tail, D - 32 * k, 1) if k else tail, stage[spot, :])
        return carry

    lax.fori_loop(0, DEV, pack, 0, unroll=8)


def dispatch(vectors, assignment, slot):
    arrays = (vectors, assignment.reshape(TOK // LANES, LANES), slot.reshape(TOK // LANES, LANES))
    return pl.pallas_call(
        dispatch_kernel,
        out_shape=jax.ShapeDtypeStruct((DEV * BLOCK, LANES), jnp.float32),
        in_specs=[pl.BlockSpec(memory_space=pltpu.HBM)] * 3,
        out_specs=VMEM,
        scratch_shapes=[
            pltpu.VMEM((D, TOK), jnp.float32),
            pltpu.VMEM((TOK // LANES, LANES), jnp.int32),
            pltpu.VMEM((TOK // LANES, LANES), jnp.int32),
            pltpu.VMEM((TOK, LANES), jnp.float32),
            pltpu.VMEM((DEV * (BLOCK + SEND - MAIN), LANES), jnp.float32),
            pltpu.VMEM((TOK // LANES, LANES), jnp.int32),
            pltpu.SMEM((TOK // LANES, LANES), jnp.int32),
            pltpu.SemaphoreType.DMA((4,)),
        ],
        compiler_params=pltpu.CompilerParams(vmem_limit_bytes=GRANT),
        name="dispatch",
    )(*(pltpu.with_memory_space_constraint(x, pltpu.HBM) for x in arrays))


def place_kernel(got_ref, old_ref, prior_ref, res_hbm, stat_ref, energy_hbm, energy_ref, res_ref, cells, tails, lab_v, lab_s, sem, out_sem):
    f32, i32 = jnp.float32, jnp.int32
    lab_v[...] = got_ref[pl.ds(MAIN, DEV, stride=BLOCK), :].astype(i32)
    copy = pltpu.make_async_copy(lab_v, lab_s, sem)
    copy.start()
    cells[...] = jnp.full(cells.shape, jnp.inf, f32)
    near = lax.broadcasted_iota(i32, (8, LANES), 1)

    def unpack(d, carry):
        first, second, third = (
            pltpu.roll(got_ref[pl.ds(d * BLOCK + 8 * k, 8), :], 32 * k + 32, 1) for k in range(MAIN // 8)
        )
        tail = jnp.where(near < 32, first, jnp.where(near < 64, second, third))
        tails[pl.ds(pl.multiple_of(d * (SEND - MAIN), 8), 8), :] = tail
        return carry

    lax.fori_loop(0, DEV, unpack, 0, unroll=8)
    copy.wait()

    def move(d, carry):
        for r in range(MAIN):
            cells[pl.ds(lab_s[d, r], 1), :] = got_ref[pl.ds(d * BLOCK + r, 1), :]
        for r in range(MAIN, SEND):
            cells[pl.ds(lab_s[d, r], 1), :] = tails[pl.ds(d * (SEND - MAIN) + r - MAIN, 1), :]
        return carry

    lax.fori_loop(0, DEV, move, 0, unroll=True)
    lane = lax.broadcasted_iota(i32, (D, LANES), 1)
    to_lane = jnp.bitwise_and(lane, 15) * 8 + lax.shift_right_logical(lane, 4)
    total = jnp.zeros((8, LANES), f32)
    outs = []
    gathered = []
    part = 2

    def send(h, planes):
        outs.append(
            pltpu.make_async_copy(res_ref.at[h, planes], res_hbm.at[h, planes], out_sem.at[len(outs)])
        )
        outs[-1].start()

    for h in range(LISTS // LANES):
        span = slice(h * LANES, (h + 1) * LANES)
        sums = jnp.zeros((D, LANES), f32)
        counts = jnp.zeros((1, LANES), f32)
        seen = []
        for j in range(CAP):
            start = j * LISTS + h * LANES
            block = cells[start : start + LANES, :].T[:D]
            full = block[:1] < jnp.inf
            block = jnp.where(full, block, 0.0)
            here = jnp.where(full, 1.0, 0.0)
            sums = sums + block
            counts = counts + here
            seen.append(here)
            res_ref[h, j] = block
            if j % part == part - 1:
                send(h, slice(j + 1 - part, j + 1))
        prior8 = jnp.broadcast_to(prior_ref[:, span].astype(f32), (8, LANES))
        prior = jnp.take_along_axis(prior8, to_lane[:8], axis=1)[:1]
        old = jnp.take_along_axis(old_ref[:, span], to_lane, axis=1)
        weight = prior + counts
        cent = (prior * old + sums) / weight
        res_ref[h, CAP] = cent
        res_ref[h, CAP + 1, :CAP] = jnp.concatenate(seen, axis=0)
        res_ref[h, CAP + 1, CAP:] = jnp.zeros((D - CAP, LANES), f32)
        stat_ref[:, span] = jnp.concatenate([prior, weight, jnp.zeros((6, LANES), f32)], axis=0)
        send(h, slice(CAP, CAP + 2))
        gathered.append((cent, seen))
    for h, (cent, seen) in enumerate(gathered):
        span = slice(h * LANES, (h + 1) * LANES)
        for j in range(CAP):
            res = res_ref[h, j] - cent * seen[j]
            square = res * res
            for t in range(D // 8):
                total = total + square[8 * t : 8 * t + 8]
    energy_ref[...] = jnp.broadcast_to(jnp.sum(total, axis=0, keepdims=True), (DEV, LANES))
    outs.append(pltpu.make_async_copy(energy_ref, energy_hbm, out_sem.at[len(outs)]))
    outs[-1].start()
    for out in outs:
        out.wait()


def place(got, old_centroids, prior_counts):
    f32 = jnp.float32
    return pl.pallas_call(
        place_kernel,
        out_shape=(
            pltpu.HBM((LISTS // LANES, CAP + 2, D, LANES), f32),
            jax.ShapeDtypeStruct((8, LISTS), f32),
            pltpu.HBM((DEV, LANES), f32),
        ),
        in_specs=[VMEM] * 3,
        out_specs=(HBM, VMEM, HBM),
        scratch_shapes=[
            pltpu.VMEM((DEV, LANES), f32),
            pltpu.VMEM((LISTS // LANES, CAP + 2, D, LANES), f32),
            pltpu.VMEM((CELLS + 8, LANES), f32),
            pltpu.VMEM((DEV * (SEND - MAIN), LANES), f32),
            pltpu.VMEM((DEV, LANES), jnp.int32),
            pltpu.SMEM((DEV, LANES), jnp.int32),
            pltpu.SemaphoreType.DMA,
            pltpu.SemaphoreType.DMA((19,)),
        ],
        compiler_params=pltpu.CompilerParams(vmem_limit_bytes=GRANT),
        name="place",
    )(got, old_centroids, prior_counts.reshape(1, LISTS))


def weave(parts, lane):
    parts = list(parts)
    for bit in (8, 4, 2, 1):
        low = jnp.bitwise_and(lane, bit) == 0
        for j in range(CAP):
            if j & bit == 0:
                one, two = parts[j], parts[j | bit]
                parts[j] = jnp.where(low, one, pltpu.roll(two, bit, 1))
                parts[j | bit] = jnp.where(low, pltpu.roll(one, LANES - bit, 1), two)
    return parts


def times(left, i, right):
    total = left[i, 0:1, :] * right[0]
    for k in range(1, CAP):
        total = total + left[i, k : k + 1, :] * right[k]
    return total


def gram_kernel(res_hbm, woven_ref, out_ref, gram_ref, next_ref, res_ref, sem):
    f32, i32 = jnp.float32, jnp.int32
    get = pltpu.make_async_copy(res_hbm, res_ref, sem)
    get.start()
    get.wait()
    lane = lax.broadcasted_iota(i32, (D, LANES), 1)
    to_list = jnp.bitwise_and(lane, 7) * 16 + lax.shift_right_logical(lane, 3)
    for h in range(LISTS // LANES):
        span = slice(h * LANES, (h + 1) * LANES)
        cent = res_ref[h, CAP]
        out_ref[:, span] = jnp.take_along_axis(cent, to_list, axis=1)
        for j in range(CAP):
            res_ref[h, j] = res_ref[h, j] - cent * res_ref[h, CAP + 1, j : j + 1]

    def row(i, carry):
        for h in range(LISTS // LANES):
            span = slice(h * LANES, (h + 1) * LANES)
            left = res_ref[h, i]
            for step in range(CAP // 2 + 1):
                j = jnp.bitwise_and(i + step, CAP - 1)
                value = jnp.sum(left * res_ref[h, j], axis=0, keepdims=True)
                gram_ref[h, i, pl.ds(j, 1), :] = value
                gram_ref[h, j, pl.ds(i, 1), :] = value
        return carry

    lax.fori_loop(0, CAP, row, 0)

    def spread(t, carry):
        tile = pl.ds(pl.multiple_of(t * 8, 8), 8)
        for h in range(LISTS // LANES):
            span = slice(h * LANES, (h + 1) * LANES)
            parts = weave([res_ref[h, j, tile, :] for j in range(CAP)], lane[:8])
            for j in range(CAP):
                at = (h * CAP + j) * LANES
                woven_ref[tile, at : at + LANES] = parts[j]
        return carry

    lax.fori_loop(0, D // 8, spread, 0)
    group = 4
    for h in range(LISTS // LANES):
        trace = gram_ref[h, 0, 0:1, :]
        for i in range(1, CAP):
            trace = trace + gram_ref[h, i, i : i + 1, :]
        trace = jnp.where(trace > 0.0, trace, 1.0)
        woven_ref[D + POWERS * CAP :, h * LANES : (h + 1) * LANES] = jnp.broadcast_to(trace, (8, LANES))
        unit = 1.0 / trace
        base = []
        for i in range(CAP):
            row = gram_ref[h, i] * unit
            base.append(row)
            next_ref[0, i] = row
            at = (h * CAP + i) * LANES
            woven_ref[D : D + CAP, at : at + LANES] = row

        def raise_rows(block, carry, h=h, base=base):
            spots = [block * group + g for g in range(group)]
            for power in range(1, POWERS):
                for i in spots:
                    row = times(next_ref.at[power - 1], i, base)
                    if power < POWERS - 1:
                        next_ref[power, i] = row
                    at = pl.multiple_of((h * CAP + i) * LANES, LANES)
                    woven_ref[D + power * CAP : D + (power + 1) * CAP, pl.ds(at, LANES)] = row
            return carry

        lax.fori_loop(0, CAP // group, raise_rows, 0)


def gram(res):
    f32 = jnp.float32
    return pl.pallas_call(
        gram_kernel,
        out_shape=(
            jax.ShapeDtypeStruct((D + POWERS * CAP + 8, CELLS), f32),
            jax.ShapeDtypeStruct((D, LISTS), f32),
        ),
        in_specs=[HBM],
        out_specs=(VMEM,) * 2,
        scratch_shapes=[
            pltpu.VMEM((LISTS // LANES, CAP, CAP, LANES), f32),
            pltpu.VMEM((POWERS - 1, CAP, CAP, LANES), f32),
            pltpu.VMEM((LISTS // LANES, CAP + 2, D, LANES), f32),
            pltpu.SemaphoreType.DMA,
        ],
        cost_estimate=pl.CostEstimate(flops=2 * CAP * CAP * D * LISTS, bytes_accessed=8 * CAP * D * LISTS, transcendentals=0),
        compiler_params=pltpu.CompilerParams(vmem_limit_bytes=GRANT),
        name="gram",
    )(pltpu.with_memory_space_constraint(res, pltpu.HBM))


def whiten_kernel(woven_ref, stat_ref, energy_ref, out_hbm, t_ref, z_ref, s_ref, q_ref, w_ref, out_ref, sem):
    f32, bf16, i32 = jnp.float32, jnp.bfloat16, jnp.int32
    group = 4
    row_of = lax.broadcasted_iota(i32, (CAP, LANES), 0)
    energy = jnp.sum(energy_ref[...], axis=(0, 1), keepdims=True)
    shrinkage = shrink_weight * energy / TOTAL + epsilon
    for h in range(LISTS // LANES):
        span = slice(h * LANES, (h + 1) * LANES)
        prior, weight = stat_ref[0:1, span], stat_ref[1:2, span]
        trace = woven_ref[D + POWERS * CAP : D + POWERS * CAP + 1, span]
        share = 1.0 / weight
        ridge = shrinkage * prior * share
        trace = trace * share

        def power(k, i):
            at = (h * CAP + i) * LANES
            return woven_ref[D + k * CAP : D + (k + 1) * CAP, at : at + LANES]

        frob = jnp.zeros((CAP, LANES), f32)
        for i in range(CAP):
            row = trace * power(0, i) + jnp.where(row_of == i, ridge, 0.0)
            frob = frob + row * row
        frob = jnp.sqrt(jnp.sum(frob, axis=0, keepdims=True) + TAIL * (ridge * ridge))
        scale = 1.0 / frob
        a, x = trace * scale, ridge * scale
        t0 = x * (2.25 + x * (0.25 * x - 1.5))
        t1 = a * (2.25 + x * (0.75 * x - 3.0))
        t2 = a * a * (0.75 * x - 1.5)
        t3 = a * a * a * 0.25
        z0 = 2.25 + x * (-2.4375 + x * (1.6875 + x * (0.0625 * x - 0.5625)))
        z1 = a * (-2.4375 + x * (3.375 + x * (0.25 * x - 1.6875)))
        z2 = a * a * (1.6875 + x * (0.375 * x - 1.6875))
        z3 = a * a * a * (0.25 * x - 0.5625)
        z4 = a * a * (a * a) * 0.0625
        middle = []
        for i in range(CAP):
            own = row_of == i
            h1, h2, h3, h4 = (power(k, i) for k in range(POWERS))
            row = t1 * h1 + t2 * h2 + t3 * h3 + jnp.where(own, t0, 0.0)
            t_ref[i] = row
            z_ref[i] = z1 * h1 + z2 * h2 + z3 * h3 + z4 * h4 + jnp.where(own, z0, 0.0)
            middle.append(jnp.where(own, 1.5, 0.0) - 0.5 * row)
        root = 1.0 / jnp.sqrt(frob)

        for step in range(1, STEPS):

            def advance(block, carry, step=step, middle=middle, root=root, h=h):
                spots = [block * group + g for g in range(group)]
                if step < STEPS - 1:
                    for i in spots:
                        s_ref[i] = times(t_ref, i, middle)
                if step > 1:
                    for i in spots:
                        moved = times(z_ref, i, middle)
                        if step == STEPS - 1:
                            q_ref[h, i] = moved * root
                        else:
                            z_ref[i] = moved
                if step < STEPS - 1:
                    for i in spots:
                        t_ref[i] = times(s_ref, i, middle)
                return carry

            lax.fori_loop(0, CAP // group, advance, 0)
            if step < STEPS - 1:
                middle = [jnp.where(row_of == i, 1.5, 0.0) - 0.5 * t_ref[i] for i in range(CAP)]

    lane = lax.broadcasted_iota(i32, (CAP, LANES), 1)
    for h in range(LISTS // LANES):
        for j, part in enumerate(weave([q_ref[h, i] for i in range(CAP)], lane)):
            w_ref[h * CAP + j] = part
    wide = 2 * LANES
    block = lax.broadcasted_iota(i32, (LANES, LANES), 0) // CAP == lax.broadcasted_iota(i32, (LANES, LANES), 1) // CAP
    empty = jnp.zeros((LANES, LANES), bf16)

    def diagonal(first, second):
        first, second = (
            jnp.where(block, jnp.concatenate([x] * (LANES // CAP), axis=0), 0.0).astype(bf16) for x in (first, second)
        )
        return jnp.concatenate(
            [jnp.concatenate([first, empty], axis=1), jnp.concatenate([empty, second], axis=1)], axis=0
        )

    copies = []
    for g in range(CELLS // wide):
        span = slice(g * wide, (g + 1) * wide)
        pair = [w_ref[2 * g], w_ref[2 * g + 1]]
        coarse = [x.astype(bf16).astype(f32) for x in pair]
        fine = [x - y for x, y in zip(pair, coarse)]
        coarse, fine = diagonal(*coarse), diagonal(*fine)
        value = woven_ref[:D, span]
        high = value.astype(bf16)
        low = (value - high.astype(f32)).astype(bf16)
        both = jnp.dot(jnp.concatenate([high, low], axis=0), coarse, preferred_element_type=f32)
        out_ref[:, span] = both[:D] + both[D:] + jnp.dot(high, fine, preferred_element_type=f32)
        copies.append(pltpu.make_async_copy(out_ref.at[:, span], out_hbm.at[:, span], sem.at[g]))
        copies[g].start()
    for copy in copies:
        copy.wait()


def whiten(woven, stat, energy):
    f32 = jnp.float32
    return pl.pallas_call(
        whiten_kernel,
        out_shape=jax.ShapeDtypeStruct((D, CELLS), f32),
        in_specs=[VMEM] * 3,
        out_specs=pl.BlockSpec(memory_space=pltpu.HBM),
        scratch_shapes=[pltpu.VMEM((CAP, CAP, LANES), f32)] * 3
        + [
            pltpu.VMEM((LISTS // LANES, CAP, CAP, LANES), f32),
            pltpu.VMEM((CELLS // LANES, CAP, LANES), f32),
            pltpu.VMEM((D, CELLS), f32),
            pltpu.SemaphoreType.DMA((CELLS // (2 * LANES),)),
        ],
        compiler_params=pltpu.CompilerParams(vmem_limit_bytes=GRANT),
        name="whiten",
    )(woven, stat, energy)


def local(vectors, assignment, slot, old_centroids, prior_counts):
    outgoing = dispatch(vectors, assignment, slot).reshape(DEV, 1, BLOCK * LANES)
    incoming = lax.all_to_all(outgoing, AXES, split_axis=0, concat_axis=0, tiled=True)
    res, stat, energy = place(incoming.reshape(DEV * BLOCK, LANES), old_centroids, prior_counts)
    shared = lax.all_to_all(energy.reshape(DEV, 1, LANES), AXES, split_axis=0, concat_axis=0, tiled=True)
    woven, centroids = gram(res)
    rotated = whiten(woven, stat, shared.reshape(DEV, LANES))
    return (centroids, rotated)


def solution(mesh):
    placed = (
        P(None, AXES),
        P(AXES),
        P(AXES),
        P(None, AXES),
        P(AXES),
    )
    return jax.shard_map(
        local,
        mesh=mesh,
        in_specs=placed,
        out_specs=(P(None, AXES), P(None, AXES)),
        check_vma=False,
    )
```
